32 devices in a mesh: rows: 8 (over z, y), scen: 4 (over x, core).
Axes of the slice: x: 2, y: 2, z: 4, core: 2. Of those that a mesh axis runs over, the one named last changes fastest.
Arguments:
- inverse: bfloat16 [4096, 16384], P('scen', 'rows'), as said below
- voltage_prev: float32 [64, 16384], P('scen', 'rows'), may hold values from -6 to 6
- line_delay: int32 [8, 16], P('rows'), may hold values from 0 to 4, as said below
- line_bus: int32 [8, 16], P('rows'), may hold values from 0 to 2047
- line_impedance: float32 [8, 16], P('rows'), may hold values from 0.5 to 2, as said below
- line_past: float32 [4, 2, 64, 8, 16], P(None, None, 'scen', 'rows'), may hold values from -6 to 6
- model_dest: int32 [1024, 1], P('rows'), may hold values from 0 to 7; in each aligned block of 128 rows (0 to 127, 128 to 255, ...) at most 32 rows name the same one
- model_bus: int32 [1024], P('rows'), may hold values from 0 to 2047
- model_gain: float32 [1024], P('rows'), may hold values from 0.3 to 3
- model_lag: float32 [1024], P('rows'), may hold values from 0.1 to 0.9
- model_state: float32 [64, 1024], P('scen', 'rows'), may hold values from -6 to 6
- model_source: float32 [6, 64, 1024], P(None, 'scen', 'rows'), may hold values from -6 to 6
- switch_bus: int32 [2, 64, 4], P(None, 'scen'), may hold values from 0 to 4095, as said below
- switch_admittance: float32 [64, 4], P('scen'), may hold values from 0.5 to 4
Outputs:
- voltage: float32 [64, 16384], P('scen', 'rows')
- model_current: float32 [64, 1024], P('scen', 'rows')
The draws below stay inside these ranges and needn't reach their ends.
Inputs may be any that keep to these rules, and one draw needn't show every extreme that they name: `line_delay`: A line joins end (p, q * 2 + c) with end (q, p * 2 + c), with the same delay and impedance at both ends; no line joins the two devices of one subnetwork; delays of lines run from 2 to 4. `line_impedance`: equal at both ends of a line. `switch_bus`: the two buses of a switched branch differ. `inverse`: each block of 4096 columns is symmetric. `model_dest`: among the models of one index of rows at most 32 name the same index.
All inputs are finite; a program needn't handle non-finite values.
Results may differ from the reference program's by a relative error of at most 0.0024.
The reference program's roundings to bfloat16 on the way (of `feed`) count: a program that leaves them out, or rounds other values in their place, can miss the bound.
Values may be sent and summed in bfloat16 or wider, within the bound.
A program may use at most 128 MiB of HBM per device.

```python
import math
import jax
import jax.numpy as jnp
import numpy as np
from jax import lax

NSUB = 4096
MOD_DEV = 128
STEPS = 6
DMAX = 4
LINE_SLOTS = 2
ROWS_DEV = 2048
SUBS = 4
NB = 16384
SCEN = 64
NMOD = 1024
INJ_SLOTS = 32
N_ROWS = 8


def symmetric_pairs(values):
    places = jnp.arange(N_ROWS, dtype=jnp.int32)
    upper = places[:, None] < places[None, :]
    flipped = jnp.swapaxes(values, 0, 1)
    return jnp.where(upper[:, :, None], values, flipped)


def draw_line_delay(key, part):
    key_live, key_delay = jax.random.split(jax.random.fold_in(key, 11))
    live = jax.random.randint(key_live, (N_ROWS, N_ROWS, LINE_SLOTS), 0, 2)
    delays = jax.random.randint(key_delay, (N_ROWS, N_ROWS, LINE_SLOTS), 2, DMAX + 1)
    places = jnp.arange(N_ROWS, dtype=jnp.int32)
    apart = places[:, None] // 2 != places[None, :] // 2
    delays = jnp.where(apart[:, :, None] & (live == 1), delays, 0)
    delays = symmetric_pairs(delays)
    delays = delays.at[0, 2, 0].set(DMAX).at[2, 0, 0].set(DMAX)
    delays = delays.at[0, 2, 1].set(2).at[2, 0, 1].set(2)
    far_pair = places[None, :] == (places[:, None] + N_ROWS // 2) % N_ROWS
    slot_ids = jnp.arange(LINE_SLOTS, dtype=jnp.int32)
    far_delay = jnp.where(slot_ids == 0, 2, DMAX).astype(jnp.int32)
    delays = jnp.where(far_pair[:, :, None], far_delay[None, None, :], delays)
    return delays.reshape(N_ROWS, N_ROWS * LINE_SLOTS).astype(jnp.int32)


def draw_line_impedance(key, part):
    unit = jax.random.uniform(jax.random.fold_in(key, 23), (N_ROWS, N_ROWS, LINE_SLOTS), jnp.float32)
    values = 0.5 * jnp.exp(unit * math.log(4.0))
    values = symmetric_pairs(values)
    return values.reshape(N_ROWS, N_ROWS * LINE_SLOTS).astype(jnp.float32)


def draw_switch_bus(key, part):
    key_first, key_step = jax.random.split(jax.random.fold_in(key, 37))
    first = jax.random.randint(key_first, (SCEN, SUBS), 0, NSUB)
    offset = jax.random.randint(key_step, (SCEN, SUBS), 1, NSUB)
    second = (first + offset) % NSUB
    return jnp.stack([first, second]).astype(jnp.int32)


def draw_inverse(key, part):
    key_base, key_diag = jax.random.split(jax.random.fold_in(key, 5))
    places = jnp.arange(NSUB, dtype=jnp.int32)
    identity = (places[:, None] == places[None, :]).astype(jnp.float32)

    def one_block(g):
        base = jax.random.normal(jax.random.fold_in(key_base, g), (NSUB, NSUB), jnp.float32)
        coupling = (base + jnp.swapaxes(base, 0, 1)) * (0.3 / math.sqrt(2.0 * NSUB))
        diagonal = jax.random.uniform(jax.random.fold_in(key_diag, g), (NSUB,), jnp.float32, 1.0, 2.0)
        return (coupling + diagonal[:, None] * identity).astype(jnp.bfloat16)
    blocks = lax.map(one_block, jnp.arange(SUBS, dtype=jnp.int32))
    return jnp.transpose(blocks, (1, 0, 2)).reshape(NSUB, NB)


def set_ends(values, rng, least, largest):
    dims = values.shape
    spot = [jax.random.randint(jax.random.fold_in(rng, axis), (), 0, dims[axis]) for axis in range(len(dims))]
    values = values.at[tuple(spot)].set(least)
    longest = dims.index(max(dims))
    spot[longest] = (spot[longest] + 1) % dims[longest]
    return values.at[tuple(spot)].set(largest)


def shard_levels(stream_key, shape, cuts, least, largest):
    level, own = 1.0, jax.random.fold_in(stream_key, 6)
    for axis_at, parts in cuts:
        draws = jnp.exp(jax.random.uniform(jax.random.fold_in(own, axis_at), (parts,), jnp.float32, least / len(cuts), largest / len(cuts)))
        level = level * jnp.repeat(draws, shape[axis_at] // parts).reshape([-1 if axis == axis_at else 1 for axis in range(len(shape))])
    return level


def shared_out(key, own, number, rows, count, top, most, lean):
    order = jax.random.permutation(key, count)
    heavy_load, ordinary = shares(count, rows * top, most, lean, True), shares(count, rows * top, most, lean, False)
    places = jnp.arange(count)

    def named(tallies, offset_by):
        used = int((tallies > 0).sum())
        fixed = max(1, used // 4)
        shifted = fixed + (places - fixed + offset_by * (used - fixed)) % max(1, count - fixed)
        return jnp.zeros((count,), jnp.int32).at[order[jnp.where(places < fixed, places, shifted)]].set(jnp.asarray(tallies, jnp.int32))

    tallies = jnp.where(number % 4 == 0, named(heavy_load, number // 4), named(ordinary, number - number // 4 - 1))
    mixed = jax.random.permutation(jax.random.fold_in(own, 3), count)
    giver, receiver = mixed[0:count // 2 * 2:2], mixed[1:count // 2 * 2:2]
    room = jnp.minimum(tallies[giver] - 1, most - tallies[receiver]) // 2
    room = jnp.where((giver == order[0]) | (receiver == order[0]) | (tallies[receiver] == 0), 0, jnp.maximum(room, 0))
    shifted = jax.random.randint(jax.random.fold_in(own, 4), (count // 2,), 0, 1 << 20) % (room + 1)
    tallies = tallies.at[giver].add(-shifted).at[receiver].add(shifted)
    items = jnp.searchsorted(jnp.cumsum(tallies), jnp.arange(rows * top), side="right").astype(jnp.int32)
    table = items.reshape(top, rows).T
    table = table[jax.random.permutation(jax.random.fold_in(own, 1), rows)]
    offset_by = jax.random.randint(jax.random.fold_in(own, 2), (rows, 1), 0, top)
    return jnp.take_along_axis(table, (jnp.arange(top)[None, :] + offset_by) % top, axis=1)


def shares(amount, total, bound, skew, full):
    weights = [(1 << 20) // math.isqrt(rank ** skew) + 1 for rank in range(1, amount + 1)]
    largest = bound if full else min(bound, max(-(-total // amount), total * weights[0] // sum(weights)))
    least = 1 if total - largest >= amount - 1 else 0
    given, surplus = [largest] + [least] * (amount - 1), total - largest - least * (amount - 1)
    while surplus > 0:
        free = [i for i in range(1, amount) if given[i] < largest] or [i for i in range(1, amount) if given[i] < bound]
        pool, remaining = sum([weights[i] for i in free]), surplus
        for i in free:
            addition = min(bound - given[i], max(1, remaining * weights[i] // pool), surplus)
            given[i] = given[i] + addition
            surplus = surplus - addition
    return np.array(given)


def normal_values(stream_key, shape, spread, bound, cuts=(), held_as=jnp.bfloat16):
    values = spread * jax.random.normal(stream_key, shape, jnp.float32)
    if cuts:
        values = values * shard_levels(stream_key, shape, cuts, -0.22, 0.18)
    return jnp.clip(values, -bound, bound).astype(held_as)


def setup_inputs(seed: int = 0) -> dict:
    arg_keys = jax.random.split(jax.random.key(seed), 15)
    inverse = draw_inverse(jax.random.fold_in(arg_keys[14], 71), 0)
    voltage_prev = normal_values(arg_keys[1], (SCEN, NB), 1.0, 6.0, ((0, 4), (1, 8)), jnp.float32)
    line_delay = draw_line_delay(jax.random.fold_in(arg_keys[14], 71), 0)
    line_bus = set_ends(jax.random.randint(arg_keys[3], (N_ROWS, N_ROWS * LINE_SLOTS), 0, ROWS_DEV), jax.random.fold_in(arg_keys[3], 1), 0, ROWS_DEV - 1).astype(jnp.int32)
    line_impedance = draw_line_impedance(jax.random.fold_in(arg_keys[14], 71), 0)
    line_past = normal_values(arg_keys[5], (DMAX, 2, SCEN, N_ROWS, N_ROWS * LINE_SLOTS), 1.0, 6.0, ((2, 4), (3, 8)), jnp.float32)
    model_dest_keys = jax.random.split(jax.random.fold_in(arg_keys[6], 1), NMOD // MOD_DEV)
    model_dest_turns = jax.random.permutation(jax.random.fold_in(arg_keys[6], 3), NMOD // MOD_DEV)
    model_dest = jax.vmap(lambda own, number: shared_out(jax.random.fold_in(arg_keys[6], 2), own, number, MOD_DEV, N_ROWS, 1, INJ_SLOTS, 2))(model_dest_keys, model_dest_turns).reshape((NMOD, 1))
    model_bus = set_ends(jax.random.randint(arg_keys[7], (NMOD,), 0, ROWS_DEV), jax.random.fold_in(arg_keys[7], 1), 0, ROWS_DEV - 1).astype(jnp.int32)
    model_gain = jnp.clip(jnp.exp(math.log(3.0) - 2.3025851 * jax.random.uniform(arg_keys[8], (NMOD,), jnp.float32) ** shard_levels(arg_keys[8], (NMOD,), ((0, 8),), -0.2, 0.2)), 0.3, 3.0)
    model_lag = jnp.clip(0.1 + 0.79999997 * jax.random.uniform(arg_keys[9], (NMOD,), jnp.float32) ** shard_levels(arg_keys[9], (NMOD,), ((0, 8),), -0.2, 0.2), 0.1, 0.9)
    model_state = normal_values(arg_keys[10], (SCEN, NMOD), 1.0, 6.0, ((0, 4), (1, 8)), jnp.float32)
    model_source = normal_values(arg_keys[11], (STEPS, SCEN, NMOD), 1.0, 6.0, ((1, 4), (2, 8)), jnp.float32)
    switch_bus = draw_switch_bus(jax.random.fold_in(arg_keys[14], 71), 0)
    switch_admittance = jnp.clip(jnp.exp(math.log(4.0) - 2.0794415 * jax.random.uniform(arg_keys[13], (SCEN, SUBS), jnp.float32) ** shard_levels(arg_keys[13], (SCEN, SUBS), ((0, 4),), -0.2, 0.2)), 0.5, 4.0)
    return dict(inverse=inverse, voltage_prev=voltage_prev, line_delay=line_delay, line_bus=line_bus, line_impedance=line_impedance, line_past=line_past, model_dest=model_dest, model_bus=model_bus, model_gain=model_gain, model_lag=model_lag, model_state=model_state, model_source=model_source, switch_bus=switch_bus, switch_admittance=switch_admittance)


def solve_all(rhs, inv3):
    def one_sub(g):
        block = lax.dynamic_index_in_dim(inv3, g, axis=1, keepdims=False).astype(jnp.float32)
        part_rhs = lax.dynamic_index_in_dim(rhs, g, axis=1, keepdims=False)
        return jnp.dot(part_rhs, block, precision=lax.Precision.HIGHEST)
    result = lax.map(one_sub, jnp.arange(SUBS, dtype=jnp.int32))
    return jnp.swapaxes(result, 0, 1)


def reference(inverse, voltage_prev, line_delay, line_bus, line_impedance, line_past, model_dest, model_bus, model_gain, model_lag, model_state, model_source, switch_bus, switch_admittance):
    inv3 = inverse.reshape(NSUB, SUBS, NSUB)
    sub_ids = jnp.arange(SUBS, dtype=jnp.int32)[None, :]
    first = switch_bus[0]
    second = switch_bus[1]
    picked_first = jnp.transpose(inv3[:, sub_ids, first], (1, 2, 0)).astype(jnp.float32)
    picked_second = jnp.transpose(inv3[:, sub_ids, second], (1, 2, 0)).astype(jnp.float32)
    branch = picked_first - picked_second
    depth = jnp.take_along_axis(branch, first[:, :, None], axis=2)[:, :, 0] - jnp.take_along_axis(branch, second[:, :, None], axis=2)[:, :, 0]
    targets = (model_dest[:, 0] * ROWS_DEV + model_bus).astype(jnp.int32)
    end_index = (jnp.arange(N_ROWS, dtype=jnp.int32)[:, None] * ROWS_DEV + line_bus).astype(jnp.int32)
    history = [line_past[k] for k in range(DMAX)]
    volt = voltage_prev
    current = model_state
    for step in range(STEPS):
        seen = volt[:, targets]
        current = model_lag * current + (1.0 - model_lag) * model_gain * (model_source[step] - seen)
        feed = jnp.zeros((SCEN, NB), jnp.float32).at[:, targets].add(current)
        line_term = jnp.zeros((SCEN, N_ROWS, N_ROWS * LINE_SLOTS), jnp.float32)
        for delay in range(2, DMAX + 1):
            older = history[step - delay + DMAX]
            line_term = line_term + jnp.where(line_delay == delay, -(2.0 / line_impedance) * older[0] - older[1], 0.0)
        feed = feed.at[:, end_index].add(-line_term)
        rounded = feed.astype(jnp.bfloat16)
        rounded = lax.optimization_barrier(rounded)
        rhs = rounded.astype(jnp.float32).reshape(SCEN, SUBS, NSUB)
        base = solve_all(rhs, inv3)
        along = jnp.sum(rhs * branch, axis=2)
        factor = switch_admittance * along / (1.0 + switch_admittance * depth)
        volt = (base - factor[:, :, None] * branch).reshape(SCEN, NB)
        if step + 2 < STEPS:
            sent = jnp.stack([volt[:, end_index], line_term])
            sent = sent.reshape(2, SCEN, N_ROWS, N_ROWS, LINE_SLOTS)
            history.append(jnp.swapaxes(sent, 2, 3).reshape(2, SCEN, N_ROWS, N_ROWS * LINE_SLOTS))
    return volt, current
```

```python
import functools

import jax
import jax.numpy as jnp
from jax import lax
from jax.experimental import pallas as pl
from jax.experimental.pallas import tpu as pltpu
from jax.sharding import PartitionSpec as P


def split_dot(value, selector):
    rows = value.shape[0]
    high = value.astype(jnp.bfloat16)
    rest = value - high.astype(jnp.float32)
    middle = rest.astype(jnp.bfloat16)
    low = (rest - middle.astype(jnp.float32)).astype(jnp.bfloat16)
    stacked = jnp.concatenate([high, middle, low], 0)
    out = jnp.dot(stacked, selector, preferred_element_type=jnp.float32)
    return out[:rows] + out[rows : 2 * rows] + out[2 * rows :]


def bits(value):
    return value.bit_length() - 1


def step_kernel(
    n,
    steps,
    depth_max,
    cap,
    slots,
    pad,
    inverse_hbm,
    prev_hbm,
    delay_ref,
    end_ref,
    impedance_ref,
    past_ref,
    dest_ref,
    bus_ref,
    gain_ref,
    lag_ref,
    state_ref,
    source_ref,
    switch_ref,
    admit_ref,
    voltage_ref,
    current_ref,
    inverse_ref,
    prev_ref,
    head_out,
    head_in,
    past_out,
    past_in,
    switch_out,
    switch_in,
    bus_out,
    bus_in,
    model_out,
    model_in,
    col_sel,
    row_sel,
    narrow,
    merge,
    branch_part,
    part,
    part_in,
    side,
    side_mate,
    side_out,
    side_in,
    volt_out,
    volt_in,
    quads,
    line_rows,
    matrix,
    line_out,
    line_in,
    feed_out,
    feed_in,
    factor_out,
    factor_in,
    partial_out,
    partial_in,
    far_out,
    far_in,
    state_out,
    state_in,
    local_sems,
    sems,
):
    f32, bf16 = jnp.float32, jnp.bfloat16
    place = lax.axis_index("rows")
    share = lax.axis_index("scen")
    subs = n // 2
    subnet, half = place // 2, place % 2
    pair = place + 1 - 2 * half
    lower = half == 0
    top, core = share // 2, share % 2
    upward = top == 0
    mate, across, corner = share + 1 - 2 * core, (share + 2) % 4, 3 - share
    scen = state_ref.shape[0]
    local, width = inverse_ref.shape
    models = dest_ref.shape[1]
    ends = end_ref.shape[1]
    count = [0]

    def remote(src, dst, device):
        at = count[0]
        count[0] += 1
        return pltpu.make_async_remote_copy(
            src_ref=src,
            dst_ref=dst,
            send_sem=sems.at[at, 0],
            recv_sem=sems.at[at, 1],
            device_id=device,
            device_id_type=pl.DeviceIdType.MESH,
        )

    barrier = pltpu.get_barrier_semaphore()
    friends = [(place, mate), (place, across), (place, corner), (pair, across)]
    friends += [((place + d) % n, share) for d in range(1, n)]
    for device in friends:
        pl.semaphore_signal(barrier, inc=1, device_id=device, device_id_type=pl.DeviceIdType.MESH)
    load_inverse = pltpu.make_async_copy(inverse_hbm, inverse_ref, local_sems.at[0])
    load_inverse.start()
    load_prev = pltpu.make_async_copy(prev_hbm, prev_ref, local_sems.at[1])
    load_prev.start()

    iota = functools.partial(lax.broadcasted_iota, jnp.int32)
    group = 128 // slots
    dest_row = dest_ref[...]
    dest = jnp.broadcast_to(dest_row.astype(f32), (models, models))
    dest_col = dest.T
    same = dest == dest_col
    rows_at, lanes_at = iota((models, models), 0), iota((models, models), 1)
    rank_col = jnp.sum(jnp.where(same & (lanes_at < rows_at), 1.0, 0.0), axis=1, keepdims=True)
    dest_col = dest_col[:, 0:1].astype(jnp.int32)
    spot = (dest_col >> 1) * 256 + (dest_col & 1) * 128 + rank_col.astype(jnp.int32)
    spot = spot + (place % group) * slots
    placing = jnp.where(iota((models, subs * 256), 1) == spot, 1.0, 0.0).astype(bf16)
    bus_row = (bus_ref[...] + (dest_row & 1) * width + 1).astype(f32)
    spread = split_dot(jnp.broadcast_to(bus_row, (16, models)), placing)
    for g in range(subs):
        bus_out[g] = spread[:8, g * 256 : (g + 1) * 256]

    switch_out[...] = jnp.zeros_like(switch_out)
    named = iota((subs, scen), 0) == subnet
    for row, values in enumerate((switch_ref[0].astype(f32), switch_ref[1].astype(f32), admit_ref[...])):
        switch_out[row : row + 1, :scen] = jnp.sum(jnp.where(named, values, 0.0), axis=0, keepdims=True)
    head_out[...] = jnp.zeros_like(head_out)
    head_out[0:1, :ends] = delay_ref[...].astype(f32)
    head_out[1:2, :ends] = impedance_ref[...]
    head_out[2:3, :ends] = (end_ref[...] + half * width + 1).astype(f32)
    head = head_out[...]
    head_out[...] = jnp.where(lower, head, pltpu.roll(head, ends, 1))
    past_out[...] = jnp.zeros_like(past_out)
    past_out[:, :ends] = past_ref[...]
    past = past_out[...]
    past_out[...] = jnp.where(lower, past, pltpu.roll(past, ends, 1))

    pl.semaphore_wait(barrier, len(friends))
    moved_buses = []
    for d in range(1, n):
        to = (place + d) % n
        moved_buses.append(remote(bus_out.at[to // 2], bus_in.at[place], (to, share)))
    for copy in moved_buses:
        copy.start()
    bus_in[place] = bus_out[subnet]
    switches = [
        remote(switch_out, switch_in.at[at], (place, to)) for at, to in enumerate((across, mate, corner))
    ]
    for copy in switches:
        copy.start()
    head_copy = remote(head_out, head_in, (pair, share))
    head_copy.start()
    past_copy = remote(past_out, past_in, (pair, share))
    past_copy.start()

    lag_row = lag_ref[...]
    gain_row = (1.0 - lag_row) * gain_ref[...]
    payload = jnp.concatenate(
        [
            jnp.broadcast_to(lag_row, (8, models)),
            jnp.broadcast_to(gain_row, (8, models)),
            state_ref[...],
            source_ref[...],
        ],
        0,
    )
    quarter = payload.shape[0] // 4
    for g in range(subs):
        base = split_dot(payload, placing[:, g * 256 : (g + 1) * 256])
        for h in range(2):
            lanes = slice(h * 128, (h + 1) * 128)
            total = base[:quarter, lanes]
            for q in range(1, 4):
                total = total + pltpu.roll(base[q * quarter : (q + 1) * quarter, lanes], 32 * q, 1)
            model_out[g, :, lanes] = total
    moved_models = []
    for d in range(1, n):
        to = (place + d) % n
        moved_models.append(remote(model_out.at[to // 2], model_in.at[place], (to, share)))
    for copy in moved_models:
        copy.start()
    model_in[place] = model_out[subnet]

    for copy in switches:
        copy.wait()
    switch = switch_out[...]
    for at in range(3):
        switch = switch + pltpu.roll(switch_in[at], scen * (at + 1), 1)
    switch = jnp.concatenate([switch] * 16, 0).T
    scens = 4 * scen
    pick_a, pick_b = switch[:scens, 0:1].astype(jnp.int32), switch[:scens, 1:2].astype(jnp.int32)
    admit = switch[:scen, 2:3]
    row_ids = iota((scens, local), 1) + share * local
    picks = (jnp.where(row_ids == pick_a, 1.0, 0.0) - jnp.where(row_ids == pick_b, 1.0, 0.0)).astype(bf16)
    load_inverse.wait()
    tile = min(width, 512)
    depth_part = jnp.zeros((scens, 1), f32)
    for at in range(0, width, tile):
        piece = jnp.dot(picks, inverse_ref[:, at : at + tile], preferred_element_type=f32)
        branch_part[:, at : at + tile] = piece
        col_ids = iota((scens, tile), 1) + (half * width + at)
        signs = jnp.where(col_ids == pick_a, 1.0, 0.0) - jnp.where(col_ids == pick_b, 1.0, 0.0)
        depth_part = depth_part + jnp.sum(piece * signs, axis=1, keepdims=True)

    head_copy.wait()
    for copy in moved_buses:
        copy.wait()
    head = head_out[...] + head_in[...]
    pieces = []
    for h in range(2):
        for g in range(n // group):
            total = bus_in[g * group, :, h * 128 : (h + 1) * 128]
            for k in range(1, group):
                total = total + bus_in[g * group + k, :, h * 128 : (h + 1) * 128]
            pieces.append(total)
    pts = jnp.concatenate(pieces + [jnp.broadcast_to(head[2:3], (8, pad))], 1)
    pts_col = pts.T[:, 0:1].astype(jnp.int32) - 1
    pts = pts[0:1].astype(jnp.int32) - 1
    points = 2 * cap + pad
    cols = cap + pad
    own_pts = jnp.concatenate(
        [jnp.where(lower, pts[:, :cap], pts[:, cap : 2 * cap]), pts[:, 2 * cap :]], 1
    ) - half * width
    col_sel[...] = jnp.where(iota((width, cols), 0) == own_pts, 1.0, 0.0).astype(bf16)
    for at in range(0, local, 256):
        rows = slice(at, at + 256)
        narrow[rows, :] = jnp.dot(
            inverse_ref[rows, :], col_sel[...], preferred_element_type=f32
        ).astype(bf16)
    own_rows = jnp.concatenate(
        [jnp.where(upward, pts_col[:cap], pts_col[cap : 2 * cap]), pts_col[2 * cap :]], 0
    ) - share * local
    row_sel[...] = jnp.where(iota((cols, local), 1) == own_rows, 1.0, 0.0).astype(bf16)
    part[:cap] = jnp.dot(row_sel[:cap], narrow[...], preferred_element_type=f32).astype(bf16)
    own_ends = pl.ds(pl.multiple_of(cap + top * ends, 16), ends)
    part[cap:] = jnp.dot(row_sel[own_ends], narrow[...], preferred_element_type=f32).astype(bf16)
    part_copy = remote(part, part_in, (place, mate))
    part_copy.start()
    wide = side.shape[1]
    product = jnp.dot(picks, narrow[...], preferred_element_type=f32)
    if wide > cols:
        product = jnp.concatenate([product, jnp.zeros((scens, wide - cols), f32)], 1)
    side[...] = jnp.where(iota((scens, wide), 1) == wide - 1, depth_part, product)
    side_copy = remote(side.at[2 * scen :], side_mate, (place, mate))
    side_copy.start()
    load_prev.wait()
    volt_out[...] = split_dot(prev_ref[...], col_sel[:, :cap])
    volt_copy = remote(volt_out, volt_in, (pair, share))
    volt_copy.start()

    equal = pts == pts_col
    sub_at = iota((points, points), 0)
    leader = jnp.min(jnp.where(equal, sub_at.astype(f32), float(points)), axis=0, keepdims=True)
    leading = leader == iota((1, points), 1).astype(f32)
    merge[...] = jnp.where(equal & leading, 1.0, 0.0).astype(bf16)
    lane = iota((1, pad), 1)
    per_pair = ends // n
    partner = (lane & (ends - 1)) >> bits(per_pair)
    origin = (partner & 1) * ends + (lane >> bits(ends)) * per_pair + (lane & (per_pair - 1))
    origin = jnp.where(lane < 2 * ends, origin + subnet * (2 * per_pair), -1)
    perm = jnp.where(iota((pad, pad), 0) == origin, 1.0, 0.0).astype(bf16)
    partner = partner >> 1

    mine = top * 2 + half
    halfrows = cap // 2
    own_half = pl.ds(pl.multiple_of(core * halfrows, 16), halfrows)
    part_copy.wait()
    whole = part[...] + part_in[...]
    quads[mine] = whole[:cap, :cap]
    line_rows[mine] = whole[cap:]
    others = [(place, across), (pair, share), (pair, across)]
    theirs = [(1 - top) * 2 + half, top * 2 + 1 - half, (1 - top) * 2 + 1 - half]
    quad_copies, row_copies, sides, forwards = [], [], [], []
    for device in others:
        quad_copies.append(remote(quads.at[mine, own_half], quads.at[mine, own_half], device))
        quad_copies[-1].start()
    for device in others:
        row_copies.append(remote(line_rows.at[mine], line_rows.at[mine], device))
        row_copies[-1].start()
    side_copy.wait()
    side_out[...] = side[: 2 * scen] + side_mate[...]
    for at, device in enumerate(others):
        rows = slice(0, scen) if at == 1 else slice(scen, 2 * scen)
        sides.append(remote(side_out.at[rows], side_in.at[at], device))
        sides[-1].start()
    for at in range(3):
        quad_copies[at].wait_recv()
        there = quads.at[theirs[at], own_half]
        forwards.append(remote(there, there, (place, mate)))
        forwards[-1].start()

    for copy in sides:
        copy.wait()
    near = side_out[:scen] + side_in[0]
    far = side_in[1] + side_in[2]
    rest = near[:, cap:] + far[:, cap:]
    spare = iota((scen, pad), 1) < 2 * ends
    branch = jnp.concatenate(
        [
            jnp.where(lower, near[:, :cap], far[:, :cap]),
            jnp.where(lower, far[:, :cap], near[:, :cap]),
            jnp.where(spare, rest[:, :pad], 0.0),
        ],
        1,
    )
    depth = rest[:, wide - cap - 1 : wide - cap]
    volt_copy.wait()
    own_volt, other_volt = volt_out[...], volt_in[...]
    volt = jnp.concatenate(
        [jnp.where(lower, own_volt, other_volt), jnp.where(lower, other_volt, own_volt)], 1
    )
    delays, impedance = head[0:1], head[1:2]
    admittance = 2.0 / jnp.where(delays == 0.0, 1.0, impedance)
    past_copy.wait()
    past = past_out[...] + past_in[...]
    history = [past[k * 2 * scen : (k + 1) * 2 * scen] for k in range(depth_max)]
    for copy in moved_models:
        copy.wait()
    band_of = iota((quarter, 128), 1) >> 5
    received = [[] for _ in range(4)]
    for h in range(2):
        for g in range(n // group):
            bands = []
            for b in range(4):
                members = [g * group + k for k in range(group) if k * slots // 32 == b]
                total = model_in[members[0], :, h * 128 : (h + 1) * 128]
                for p in members[1:]:
                    total = total + model_in[p, :, h * 128 : (h + 1) * 128]
                bands.append(total)
            for q in range(4):
                total = bands[(3 - q) % 4]
                for b in range(3):
                    total = jnp.where(band_of == b, bands[(b - q) % 4], total)
                received[q].append(pltpu.roll(total, (128 - 32 * q) % 128, 1) if q else total)
    received = jnp.concatenate([jnp.concatenate(parts, 1) for parts in received], 0)
    lag, gain = received[0:1], received[8:9]
    current = received[16 : 16 + scen]
    lines = []
    homes = []
    for step in range(steps):
        current = lag * current + gain * (received[16 + (step + 1) * scen : 16 + (step + 2) * scen] - volt)
        if step + 1 == steps:
            state_out[...] = jnp.where(lower, current[:, :cap], current[:, cap:])
            for d in range(1, n):
                homes.append(remote(state_out, state_in.at[d - 1], ((place + d) % n, share)))
            for copy in homes:
                copy.start()
        if step >= 2:
            for copy in lines[step - 2]:
                copy.wait()
            merged = jnp.zeros((2 * scen, pad), f32)
            for d in range(1, subs):
                moved = split_dot(line_in[step - 2, d - 1], perm)
                merged = merged + jnp.where(partner == (subnet + subs - d) % subs, moved, 0.0)
            history.append(merged)
        line_term = jnp.zeros((scen, pad), f32)
        for delay in range(2, depth_max + 1):
            older = history[step - delay + depth_max]
            line_term = line_term + jnp.where(
                delays == delay, -admittance * older[:scen] - older[scen:], 0.0
            )
        feed = split_dot(jnp.concatenate([current, -line_term], 1), merge[...])
        rhs = feed.astype(bf16)
        along = jnp.sum(rhs.astype(f32) * branch, axis=1, keepdims=True)
        factor = admit * along / (1.0 + admit * depth)
        if step == 0:
            for copy in row_copies:
                copy.wait()
            matrix[2 * cap :, :] = jnp.zeros((pad, points), bf16)
            for x in range(2):
                rows = slice(2 * cap + x * ends, 2 * cap + (x + 1) * ends)
                for h in range(2):
                    matrix[rows, h * cap : (h + 1) * cap] = line_rows[2 * x + h, :, :cap]
                matrix[rows, 2 * cap :] = line_rows[2 * x, :, cap:] + line_rows[2 * x + 1, :, cap:]
            matrix[: 2 * cap, 2 * cap :] = matrix[2 * cap :, : 2 * cap].astype(f32).T.astype(bf16)
            for copy in quad_copies:
                copy.wait_send()
            for copy in forwards:
                copy.wait()
            for x in range(2):
                for h in range(2):
                    matrix[x * cap : (x + 1) * cap, h * cap : (h + 1) * cap] = quads[2 * x + h]
        if step + 1 < steps:
            full = jnp.dot(rhs, matrix[...], preferred_element_type=f32) - factor * branch
            volt = full[:, : 2 * cap]
        if step + 2 < steps:
            line_out[step] = jnp.concatenate([full[:, 2 * cap :], line_term], 0)
            lines.append(
                [
                    remote(
                        line_out.at[step],
                        line_in.at[step, d - 1],
                        (((subnet + d) % subs) * 2 + half, share),
                    )
                    for d in range(1, subs)
                ]
            )
            for copy in lines[step]:
                copy.start()

    near = jnp.concatenate([jnp.where(upward, rhs[:, :cap], rhs[:, cap : 2 * cap]), rhs[:, 2 * cap :]], 1)
    feed_out[0] = near
    feed_out[1] = jnp.concatenate(
        [jnp.where(upward, rhs[:, cap : 2 * cap], rhs[:, :cap]), rhs[:, 2 * cap :]], 1
    )
    factor_out[...] = jnp.broadcast_to(factor, factor_out.shape)
    shared = []
    for at, to in enumerate((across, mate, corner)):
        shared.append(remote(feed_out.at[0 if at == 1 else 1], feed_in.at[at], (place, to)))
        shared.append(remote(factor_out, factor_in.at[at], (place, to)))
    for copy in shared:
        copy.start()
    for copy in shared:
        copy.wait()
    feeds = jnp.concatenate([near] + [feed_in[at] for at in range(3)], 0)
    dense = jnp.dot(feeds, row_sel[...], preferred_element_type=f32).astype(bf16)
    factors = jnp.concatenate([factor] + [factor_in[at][:, 0:1] for at in range(3)], 0)
    to_mate, to_across = [], []

    def pass_on(at):
        to_mate[at].wait()
        columns = slice(at * tile, (at + 1) * tile)
        far_out[at] = far_out[at] + partial_in[at, scen:]
        voltage_ref[:, columns] = voltage_ref[:, columns] + partial_in[at, :scen]
        to_across.append(remote(far_out.at[at], far_in.at[at], (place, across)))
        to_across[at].start()

    tiles = width // tile
    for at in range(tiles):
        columns = slice(at * tile, (at + 1) * tile)
        product = jnp.dot(dense, inverse_ref[:, columns], preferred_element_type=f32)
        product = product - factors * branch_part[:, columns]
        partial_out[at] = product[2 * scen :]
        to_mate.append(remote(partial_out.at[at], partial_in.at[at], (place, mate)))
        to_mate[at].start()
        voltage_ref[:, columns] = product[:scen]
        far_out[at] = product[scen : 2 * scen]
        if at:
            pass_on(at - 1)
    pass_on(tiles - 1)
    for copy in homes:
        copy.wait()
    back = jnp.concatenate([state_out[...]] + [state_in[d - 1] for d in range(1, n)], 0)
    rank_row = jnp.sum(jnp.where(same & (rows_at < lanes_at), 1.0, 0.0), axis=0, keepdims=True)
    home = jnp.where(
        iota((cap, models), 0) == place * slots + rank_row.astype(jnp.int32), 1.0, 0.0
    ).astype(bf16)
    back = split_dot(back, home)
    out = jnp.zeros((scen, models), f32)
    for d in range(n):
        out = out + jnp.where(dest_row == (place + n - d) % n, back[d * scen : (d + 1) * scen], 0.0)
    current_ref[...] = out
    for at in range(tiles):
        to_across[at].wait()
        columns = slice(at * tile, (at + 1) * tile)
        voltage_ref[:, columns] = voltage_ref[:, columns] + far_in[at]


def per_device(
    inverse,
    voltage_prev,
    line_delay,
    line_bus,
    line_impedance,
    line_past,
    model_dest,
    model_bus,
    model_gain,
    model_lag,
    model_state,
    model_source,
    switch_bus,
    switch_admittance,
):
    n = lax.axis_size("rows")
    groups = lax.axis_size("scen")
    local, width = inverse.shape
    scen = voltage_prev.shape[0]
    steps = model_source.shape[0]
    ends = line_bus.shape[1]
    models = model_bus.shape[0]
    depth_max = line_past.shape[0]
    slots = max(2, 2 * models // n)
    cap = n * slots
    f32, bf16 = jnp.float32, jnp.bfloat16
    subs = n // 2
    pad = max(128, 2 * ends)
    points = 2 * cap + pad
    cols = cap + pad
    wide = cols if pad > 2 * ends else cols + 128
    past_rows = depth_max * 2 * scen
    quarter = (16 + (steps + 1) * scen) // 4
    tile = min(width, 512)
    tiles = width // tile
    copies = 3 * (n - 1) + (steps - 2) * (subs - 1) + 30 + 2 * tiles
    vmem = pl.BlockSpec(memory_space=pltpu.VMEM)
    hbm = pl.BlockSpec(memory_space=pl.ANY)
    return pl.pallas_call(
        functools.partial(step_kernel, n, steps, depth_max, cap, slots, pad),
        out_shape=(
            jax.ShapeDtypeStruct((scen, width), f32),
            jax.ShapeDtypeStruct((scen, models), f32),
        ),
        in_specs=[hbm] * 2 + [vmem] * 12,
        out_specs=(vmem, vmem),
        scratch_shapes=[
            pltpu.VMEM((local, width), bf16),
            pltpu.VMEM((scen, width), f32),
            pltpu.VMEM((8, pad), f32),
            pltpu.VMEM((8, pad), f32),
            pltpu.VMEM((past_rows, pad), f32),
            pltpu.VMEM((past_rows, pad), f32),
            pltpu.VMEM((8, 128), f32),
            pltpu.VMEM((groups - 1, 8, 128), f32),
            pltpu.VMEM((subs, 8, 256), f32),
            pltpu.VMEM((n, 8, 256), f32),
            pltpu.VMEM((subs, quarter, 256), f32),
            pltpu.VMEM((n, quarter, 256), f32),
            pltpu.VMEM((width, cols), bf16),
            pltpu.VMEM((cols, local), bf16),
            pltpu.VMEM((local, cols), bf16),
            pltpu.VMEM((points, points), bf16),
            pltpu.VMEM((groups * scen, width), f32),
            pltpu.VMEM((cap + ends, cols), bf16),
            pltpu.VMEM((cap + ends, cols), bf16),
            pltpu.VMEM((groups * scen, wide), f32),
            pltpu.VMEM((2 * scen, wide), f32),
            pltpu.VMEM((2 * scen, wide), f32),
            pltpu.VMEM((3, scen, wide), f32),
            pltpu.VMEM((scen, cap), f32),
            pltpu.VMEM((scen, cap), f32),
            pltpu.VMEM((4, cap, cap), bf16),
            pltpu.VMEM((4, ends, cols), bf16),
            pltpu.VMEM((points, points), bf16),
            pltpu.VMEM((steps - 2, 2 * scen, pad), f32),
            pltpu.VMEM((steps - 2, subs - 1, 2 * scen, pad), f32),
            pltpu.VMEM((2, scen, cols), bf16),
            pltpu.VMEM((groups - 1, scen, cols), bf16),
            pltpu.VMEM((scen, 128), f32),
            pltpu.VMEM((groups - 1, scen, 128), f32),
            pltpu.VMEM((tiles, 2 * scen, tile), f32),
            pltpu.VMEM((tiles, 2 * scen, tile), f32),
            pltpu.VMEM((tiles, scen, tile), f32),
            pltpu.VMEM((tiles, scen, tile), f32),
            pltpu.VMEM((scen, cap), f32),
            pltpu.VMEM((n - 1, scen, cap), f32),
            pltpu.SemaphoreType.DMA((2,)),
            pltpu.SemaphoreType.DMA((copies, 2)),
        ],
        compiler_params=pltpu.CompilerParams(
            collective_id=0, has_side_effects=True, vmem_limit_bytes=56 * 2**20
        ),
    )(
        inverse,
        voltage_prev,
        line_delay,
        line_bus,
        line_impedance,
        line_past.reshape(past_rows, ends),
        model_dest.reshape(1, models),
        model_bus.reshape(1, models),
        model_gain.reshape(1, models),
        model_lag.reshape(1, models),
        model_state,
        model_source.reshape(steps * scen, models),
        jnp.swapaxes(switch_bus, 1, 2),
        switch_admittance.T,
    )


def solution(mesh):
    placed = (
        P("scen", "rows"),
        P("scen", "rows"),
        P("rows", None),
        P("rows", None),
        P("rows", None),
        P(None, None, "scen", "rows", None),
        P("rows", None),
        P("rows"),
        P("rows"),
        P("rows"),
        P("scen", "rows"),
        P(None, "scen", "rows"),
        P(None, "scen", None),
        P("scen", None),
    )
    return jax.shard_map(
        per_device,
        mesh=mesh,
        in_specs=placed,
        out_specs=(P("scen", "rows"), P("scen", "rows")),
        check_vma=False,
    )
```

```python
import functools

import jax
import jax.numpy as jnp
from jax import lax
from jax.experimental import pallas as pl
from jax.experimental.pallas import tpu as pltpu
from jax.sharding import PartitionSpec as P


def split_dot(value, selector):
    rows = value.shape[0]
    high = value.astype(jnp.bfloat16)
    rest = value - high.astype(jnp.float32)
    middle = rest.astype(jnp.bfloat16)
    low = (rest - middle.astype(jnp.float32)).astype(jnp.bfloat16)
    stacked = jnp.concatenate([high, middle, low], 0)
    out = jnp.dot(stacked, selector, preferred_element_type=jnp.float32)
    return out[:rows] + out[rows : 2 * rows] + out[2 * rows :]


def bits(value):
    return value.bit_length() - 1


def step_kernel(
    n,
    steps,
    depth_max,
    cap,
    slots,
    pad,
    packed,
    inverse_hbm,
    prev_hbm,
    delay_ref,
    end_ref,
    impedance_ref,
    past_ref,
    dest_ref,
    bus_ref,
    gain_ref,
    lag_ref,
    state_ref,
    source_ref,
    switch_ref,
    admit_ref,
    voltage_ref,
    current_ref,
    inverse_ref,
    prev_ref,
    head_out,
    head_in,
    past_out,
    past_in,
    switch_out,
    switch_in,
    bus_out,
    bus_in,
    model_out,
    model_in,
    col_sel,
    row_sel,
    rows_part,
    rows_mate,
    ends_mate,
    solve,
    merge,
    branch_part,
    branch_mate,
    branch_sum,
    branch_in,
    part,
    part_in,
    side,
    side_mate,
    side_out,
    side_in,
    volt_out,
    volt_in,
    quads,
    line_rows,
    matrix,
    line_out,
    line_in,
    state_out,
    state_in,
    local_sems,
    sems,
):
    f32, bf16 = jnp.float32, jnp.bfloat16
    place = lax.axis_index("rows")
    share = lax.axis_index("scen")
    subs = n // 2
    subnet, half = place // 2, place % 2
    pair = place + 1 - 2 * half
    lower = half == 0
    top, core = share // 2, share % 2
    upward = top == 0
    mate, across, corner = share + 1 - 2 * core, (share + 2) % 4, 3 - share
    scen = state_ref.shape[0]
    local, width = inverse_ref.shape
    models = dest_ref.shape[1]
    ends = end_ref.shape[1]
    count = [0]

    def remote(src, dst, device):
        at = count[0]
        count[0] += 1
        return pltpu.make_async_remote_copy(
            src_ref=src,
            dst_ref=dst,
            send_sem=sems.at[at, 0],
            recv_sem=sems.at[at, 1],
            device_id=device,
            device_id_type=pl.DeviceIdType.MESH,
        )

    barrier = pltpu.get_barrier_semaphore()
    friends = [(place, mate), (place, across), (place, corner), (pair, across)]
    friends += [((place + d) % n, share) for d in range(1, n)]
    for device in friends:
        pl.semaphore_signal(barrier, inc=1, device_id=device, device_id_type=pl.DeviceIdType.MESH)
    load_inverse = pltpu.make_async_copy(inverse_hbm, inverse_ref, local_sems.at[0])
    load_inverse.start()
    load_prev = pltpu.make_async_copy(prev_hbm, prev_ref, local_sems.at[1])
    load_prev.start()

    iota = functools.partial(lax.broadcasted_iota, jnp.int32)
    group = 128 // slots
    dest_row = dest_ref[...]
    dest = jnp.broadcast_to(dest_row.astype(f32), (models, models))
    dest_col = dest.T
    same = dest == dest_col
    rows_at, lanes_at = iota((models, models), 0), iota((models, models), 1)
    rank_col = jnp.sum(jnp.where(same & (lanes_at < rows_at), 1.0, 0.0), axis=1, keepdims=True)
    dest_col = dest_col[:, 0:1].astype(jnp.int32)
    spot = (dest_col >> 1) * 256 + (dest_col & 1) * 128 + rank_col.astype(jnp.int32)
    spot = spot + (place % group) * slots
    placing = jnp.where(iota((models, subs * 256), 1) == spot, 1.0, 0.0).astype(bf16)
    bus_row = (bus_ref[...] + (dest_row & 1) * width + 1).astype(f32)
    spread = split_dot(jnp.broadcast_to(bus_row, (16, models)), placing)
    for g in range(subs):
        bus_out[g] = spread[:8, g * 256 : (g + 1) * 256]

    switch_out[...] = jnp.zeros_like(switch_out)
    named = iota((subs, scen), 0) == subnet
    for row, values in enumerate((switch_ref[0].astype(f32), switch_ref[1].astype(f32), admit_ref[...])):
        switch_out[row : row + 1, :scen] = jnp.sum(jnp.where(named, values, 0.0), axis=0, keepdims=True)
    head_out[...] = jnp.zeros_like(head_out)
    head_out[0:1, :ends] = delay_ref[...].astype(f32)
    head_out[1:2, :ends] = impedance_ref[...]
    head_out[2:3, :ends] = (end_ref[...] + half * width + 1).astype(f32)
    head = head_out[...]
    head_out[...] = jnp.where(lower, head, pltpu.roll(head, ends, 1))
    past_out[...] = jnp.zeros_like(past_out)
    past_out[:, :ends] = past_ref[...]
    past = past_out[...]
    past_out[...] = jnp.where(lower, past, pltpu.roll(past, ends, 1))

    pl.semaphore_wait(barrier, len(friends))
    moved_buses = []
    for d in range(1, n):
        to = (place + d) % n
        moved_buses.append(remote(bus_out.at[to // 2], bus_in.at[place], (to, share)))
    for copy in moved_buses:
        copy.start()
    bus_in[place] = bus_out[subnet]
    switches = [
        remote(switch_out, switch_in.at[at], (place, to)) for at, to in enumerate((across, mate, corner))
    ]
    for copy in switches:
        copy.start()
    head_copy = remote(head_out, head_in, (pair, share))
    head_copy.start()
    past_copy = remote(past_out, past_in, (pair, share))
    past_copy.start()

    lag_row = lag_ref[...]
    gain_row = (1.0 - lag_row) * gain_ref[...]
    payload = jnp.concatenate(
        [
            jnp.broadcast_to(lag_row, (8, models)),
            jnp.broadcast_to(gain_row, (8, models)),
            state_ref[...],
            source_ref[...],
        ],
        0,
    )
    quarter = payload.shape[0] // 4
    for g in range(subs):
        base = split_dot(payload, placing[:, g * 256 : (g + 1) * 256])
        for h in range(2):
            lanes = slice(h * 128, (h + 1) * 128)
            total = base[:quarter, lanes]
            for q in range(1, 4):
                total = total + pltpu.roll(base[q * quarter : (q + 1) * quarter, lanes], 32 * q, 1)
            model_out[g, :, lanes] = total
    moved_models = []
    for d in range(1, n):
        to = (place + d) % n
        moved_models.append(remote(model_out.at[to // 2], model_in.at[place], (to, share)))
    for copy in moved_models:
        copy.start()
    model_in[place] = model_out[subnet]

    for copy in switches:
        copy.wait()
    switch = switch_out[...]
    for at in range(3):
        switch = switch + pltpu.roll(switch_in[at], scen * (at + 1), 1)
    switch = jnp.concatenate([switch] * 16, 0).T
    scens = 4 * scen
    pick_a, pick_b = switch[:scens, 0:1].astype(jnp.int32), switch[:scens, 1:2].astype(jnp.int32)
    admit = switch[:scen, 2:3]
    row_ids = iota((scens, local), 1) + share * local
    row_sel[cap + ends :] = (
        jnp.where(row_ids == pick_a, 1.0, 0.0) - jnp.where(row_ids == pick_b, 1.0, 0.0)
    ).astype(bf16)

    head_copy.wait()
    for copy in moved_buses:
        copy.wait()
    head = head_out[...] + head_in[...]
    pieces = []
    for h in range(2):
        for g in range(n // group):
            total = bus_in[g * group, :, h * 128 : (h + 1) * 128]
            for k in range(1, group):
                total = total + bus_in[g * group + k, :, h * 128 : (h + 1) * 128]
            pieces.append(total)
    pts = jnp.concatenate(pieces + [jnp.broadcast_to(head[2:3], (8, pad))], 1)
    pts_col = pts.T[:, 0:1].astype(jnp.int32) - 1
    pts = pts[0:1].astype(jnp.int32) - 1
    points = 2 * cap + pad
    cols = cap + pad
    own_pts = jnp.concatenate(
        [jnp.where(lower, pts[:, :cap], pts[:, cap : 2 * cap]), pts[:, 2 * cap :]], 1
    ) - half * width
    col_sel[...] = jnp.where(iota((width, cols), 0) == own_pts, 1.0, 0.0).astype(bf16)
    own_rows = jnp.concatenate(
        [
            jnp.where(upward, pts_col[:cap], pts_col[cap : 2 * cap]),
            jnp.where(upward, pts_col[2 * cap : 2 * cap + ends], pts_col[2 * cap + ends : 2 * cap + 2 * ends]),
        ],
        0,
    ) - share * local
    live = cap + ends
    row_sel[:live] = jnp.where(iota((live, local), 1) == own_rows, 1.0, 0.0).astype(bf16)
    load_inverse.wait()
    tile = min(width, 512)
    for at in range(0, width, tile):
        piece = jnp.dot(row_sel[...], inverse_ref[:, at : at + tile], preferred_element_type=f32)
        rows_part[:, at : at + tile] = piece[:live].astype(bf16)
        branch_part[:, at : at + tile] = piece[live:]
    part[...] = jnp.dot(rows_part[...], col_sel[...], preferred_element_type=f32).astype(bf16)
    part_copy = remote(part, part_in, (place, mate))
    part_copy.start()
    depth_part = jnp.zeros((scens, 1), f32)
    for at in range(0, width, tile):
        col_ids = iota((scens, tile), 1) + (half * width + at)
        signs = jnp.where(col_ids == pick_a, 1.0, 0.0) - jnp.where(col_ids == pick_b, 1.0, 0.0)
        depth_part = depth_part + jnp.sum(branch_part[:, at : at + tile] * signs, axis=1, keepdims=True)
    wide = side.shape[1]
    product = split_dot(branch_part[...], col_sel[...])
    if wide > cols:
        product = jnp.concatenate([product, jnp.zeros((scens, wide - cols), f32)], 1)
    side[...] = jnp.where(iota((scens, wide), 1) == wide - 1, depth_part, product)
    side_copy = remote(side.at[2 * scen :], side_mate, (place, mate))
    side_copy.start()
    load_prev.wait()
    volt_out[...] = split_dot(prev_ref[...], col_sel[:, :cap])
    volt_copy = remote(volt_out, volt_in, (pair, share))
    volt_copy.start()
    halfrows, halfwidth = cap // 2, width // 2
    own_half = pl.ds(pl.multiple_of(core * halfrows, 16), halfrows)
    mate_half = pl.ds(pl.multiple_of((1 - core) * halfrows, 16), halfrows)
    own_lanes = pl.ds(pl.multiple_of(core * halfwidth, 128), halfwidth)
    mate_lanes = pl.ds(pl.multiple_of((1 - core) * halfwidth, 128), halfwidth)
    branch_copy = remote(branch_part.at[2 * scen :], branch_mate, (place, mate))
    rows_copy = remote(rows_part.at[mate_half], rows_mate, (place, mate))
    ends_copy = remote(rows_part.at[cap:, mate_lanes], ends_mate, (place, mate))

    equal = pts == pts_col
    sub_at = iota((points, points), 0)
    leader = jnp.min(jnp.where(equal, sub_at.astype(f32), float(points)), axis=0, keepdims=True)
    leading = leader == iota((1, points), 1).astype(f32)
    merge[...] = jnp.where(equal & leading, 1.0, 0.0).astype(bf16)
    lane = iota((1, pad), 1)
    per_pair = ends // n
    partner = (lane & (ends - 1)) >> bits(per_pair)
    origin = (partner & 1) * ends + (lane >> bits(ends)) * per_pair + (lane & (per_pair - 1))
    origin = jnp.where(lane < 2 * ends, origin + subnet * (2 * per_pair), -1)
    perm = jnp.where(iota((pad, pad), 0) == origin, 1.0, 0.0).astype(bf16)
    partner = partner >> 1
    if packed:
        way, spot = lane >> bits(2 * ends), lane & (2 * ends - 1)
        to = (subnet + way + 1) & (subs - 1)
        fellow = (spot & (ends - 1)) >> bits(per_pair)
        origin = (fellow & 1) * ends + (to * 2 + (spot >> bits(ends))) * per_pair + (spot & (per_pair - 1))
        sent = (way < subs - 1) & ((fellow >> 1) == subnet)
        spread = jnp.where(iota((pad, pad), 0) == jnp.where(sent, origin, -1), 1.0, 0.0).astype(bf16)

    mine = top * 2 + half
    part_copy.wait()
    whole = part[...] + part_in[...]
    quads[mine] = whole[:cap, :cap]
    line_rows[mine] = whole[cap:]
    others = [(place, across), (pair, share), (pair, across)]
    theirs = [(1 - top) * 2 + half, top * 2 + 1 - half, (1 - top) * 2 + 1 - half]
    quad_copies, row_copies, sides, forwards = [], [], [], []
    for device in others:
        quad_copies.append(remote(quads.at[mine, own_half], quads.at[mine, own_half], device))
        quad_copies[-1].start()
    for device in others:
        row_copies.append(remote(line_rows.at[mine], line_rows.at[mine], device))
        row_copies[-1].start()
    side_copy.wait()
    side_out[...] = side[: 2 * scen] + side_mate[...]
    for at, device in enumerate(others):
        rows = slice(0, scen) if at == 1 else slice(scen, 2 * scen)
        sides.append(remote(side_out.at[rows], side_in.at[at], device))
        sides[-1].start()
    rows_copy.start()
    ends_copy.start()
    branch_copy.start()
    rows_copy.wait()
    ends_copy.wait()
    if pad > 2 * ends:
        solve[2 * cap + 2 * ends :] = jnp.zeros((pad - 2 * ends, width), bf16)
    solve_rows = pl.ds(pl.multiple_of(top * cap + core * halfrows, 16), halfrows)
    solve_ends = pl.ds(pl.multiple_of(2 * cap + top * ends, 16), ends)
    solve[solve_rows] = rows_part[own_half] + rows_mate[...]
    solve[solve_ends, own_lanes] = rows_part[cap:, own_lanes] + ends_mate[...]
    their_rows = pl.ds(pl.multiple_of((1 - top) * cap + core * halfrows, 16), halfrows)
    their_ends = pl.ds(pl.multiple_of(2 * cap + (1 - top) * ends, 16), ends)
    spread_rows, spread_mate, spread_far = [], [], []
    for device, into in (((place, across), spread_rows), ((place, mate), spread_mate)):
        into.append(remote(solve.at[solve_rows], solve.at[solve_rows], device))
        into.append(remote(solve.at[solve_ends, own_lanes], solve.at[solve_ends, own_lanes], device))
    for copy in spread_rows:
        copy.start()
    branch_copy.wait()
    branch_sum[...] = branch_part[: 2 * scen] + branch_mate[...]
    branch_across = remote(branch_sum.at[scen:], branch_in, (place, across))
    branch_across.start()
    for at in range(3):
        quad_copies[at].wait_recv()
        there = quads.at[theirs[at], own_half]
        forwards.append(remote(there, there, (place, mate)))
        forwards[-1].start()
    for copy in spread_mate:
        copy.start()

    for copy in sides:
        copy.wait()
    near = side_out[:scen] + side_in[0]
    far = side_in[1] + side_in[2]
    rest = near[:, cap:] + far[:, cap:]
    spare = iota((scen, pad), 1) < 2 * ends
    branch = jnp.concatenate(
        [
            jnp.where(lower, near[:, :cap], far[:, :cap]),
            jnp.where(lower, far[:, :cap], near[:, :cap]),
            jnp.where(spare, rest[:, :pad], 0.0),
        ],
        1,
    )
    depth = rest[:, wide - cap - 1 : wide - cap]
    volt_copy.wait()
    own_volt, other_volt = volt_out[...], volt_in[...]
    volt = jnp.concatenate(
        [jnp.where(lower, own_volt, other_volt), jnp.where(lower, other_volt, own_volt)], 1
    )
    delays, impedance = head[0:1], head[1:2]
    admittance = 2.0 / jnp.where(delays == 0.0, 1.0, impedance)
    past_copy.wait()
    past = past_out[...] + past_in[...]
    history = []
    for k in range(depth_max):
        older = past[k * 2 * scen : (k + 1) * 2 * scen]
        history.append(-admittance * older[:scen] - older[scen:])
    branch_ends, admittance_ends = branch[:, 2 * cap :], admittance
    if packed:
        branch_ends = split_dot(branch_ends, spread)
        admittance_ends = split_dot(jnp.broadcast_to(admittance, (16, pad)), spread)[:1]
    for copy in moved_models:
        copy.wait()
    band_of = iota((quarter, 128), 1) >> 5
    received = [[] for _ in range(4)]
    for h in range(2):
        for g in range(n // group):
            bands = []
            for b in range(4):
                members = [g * group + k for k in range(group) if k * slots // 32 == b]
                total = model_in[members[0], :, h * 128 : (h + 1) * 128]
                for p in members[1:]:
                    total = total + model_in[p, :, h * 128 : (h + 1) * 128]
                bands.append(total)
            for q in range(4):
                total = bands[(3 - q) % 4]
                for b in range(3):
                    total = jnp.where(band_of == b, bands[(b - q) % 4], total)
                received[q].append(pltpu.roll(total, (128 - 32 * q) % 128, 1) if q else total)
    received = jnp.concatenate([jnp.concatenate(parts, 1) for parts in received], 0)
    lag, gain = received[0:1], received[8:9]
    current = received[16 : 16 + scen]
    lines = []
    homes = []
    for step in range(steps):
        current = lag * current + gain * (received[16 + (step + 1) * scen : 16 + (step + 2) * scen] - volt)
        if step + 1 == steps:
            state_out[...] = jnp.where(lower, current[:, :cap], current[:, cap:])
            for d in range(1, n):
                homes.append(remote(state_out, state_in.at[d - 1], ((place + d) % n, share)))
            for copy in homes:
                copy.start()
        feed = split_dot(current, merge[: 2 * cap])
        if step + 1 == steps:
            for copy in spread_rows:
                copy.wait()
            for there in (solve.at[their_rows], solve.at[their_ends, own_lanes]):
                spread_far.append(remote(there, there, (place, mate)))
                spread_far[-1].start()
        if step >= 2:
            for copy in lines[step - 2]:
                copy.wait()
            arrived = line_in[step - 2, 0]
            if packed:
                for d in range(2, subs):
                    arrived = arrived + line_in[step - 2, d - 1]
                arrived = jnp.concatenate([arrived, pltpu.roll(arrived, pad // 2, 1)], 0)
            else:
                arrived = jnp.zeros((scen, pad), f32)
                for d in range(1, subs):
                    moved = split_dot(line_in[step - 2, d - 1], perm)
                    arrived = arrived + jnp.where(partner == (subnet + subs - d) % subs, moved, 0.0)
            history.append(arrived)
        line_term = jnp.zeros((scen, pad), f32)
        for delay in range(2, depth_max + 1):
            line_term = line_term + jnp.where(delays == delay, history[step - delay + depth_max], 0.0)
        feed = feed - split_dot(line_term, merge[2 * cap :])
        rhs = feed.astype(bf16)
        term_ends = split_dot(line_term, spread) if packed else line_term
        along = jnp.sum(rhs.astype(f32) * branch, axis=1, keepdims=True)
        factor = admit * along / (1.0 + admit * depth)
        if step == 0:
            for copy in row_copies:
                copy.wait()
            matrix[2 * cap :, :] = jnp.zeros((pad, points), bf16)
            for x in range(2):
                rows = slice(2 * cap + x * ends, 2 * cap + (x + 1) * ends)
                for h in range(2):
                    matrix[rows, h * cap : (h + 1) * cap] = line_rows[2 * x + h, :, :cap]
                matrix[rows, 2 * cap :] = line_rows[2 * x, :, cap:] + line_rows[2 * x + 1, :, cap:]
            matrix[: 2 * cap, 2 * cap :] = matrix[2 * cap :, : 2 * cap].astype(f32).T.astype(bf16)
            if packed:
                matrix[:, 2 * cap :] = jnp.dot(
                    matrix[:, 2 * cap :], spread, preferred_element_type=f32
                ).astype(bf16)
            for copy in quad_copies:
                copy.wait_send()
            for copy in forwards:
                copy.wait()
            for x in range(2):
                for h in range(2):
                    matrix[x * cap : (x + 1) * cap, h * cap : (h + 1) * cap] = quads[2 * x + h]
        if step + 1 < steps:
            full = jnp.dot(rhs, matrix[...], preferred_element_type=f32)
            volt = full[:, : 2 * cap] - factor * branch[:, : 2 * cap]
        if step + 2 < steps:
            sending = -admittance_ends * (full[:, 2 * cap :] - factor * branch_ends) - term_ends
            for d in range(1, subs):
                if packed:
                    upper = pltpu.roll(sending[:8], (128 - 2 * ends * (d - 1)) % 128, 1) if d > 1 else sending[:8]
                    under = pltpu.roll(sending[8:], (64 - 2 * ends * (d - 1)) % 128, 1)
                    line_out[step, d - 1] = jnp.where(lane < 64, upper, under)
                else:
                    line_out[step, d - 1] = sending
            lines.append(
                [
                    remote(
                        line_out.at[step, d - 1],
                        line_in.at[step, d - 1],
                        (((subnet + d) % subs) * 2 + half, share),
                    )
                    for d in range(1, subs)
                ]
            )
            for copy in lines[step]:
                copy.start()

    branch_across.wait()
    for copy in spread_mate + spread_far:
        copy.wait()
    for at in range(0, width, tile):
        columns = slice(at, at + tile)
        product = jnp.dot(rhs, solve[:, columns], preferred_element_type=f32)
        voltage_ref[:, columns] = product - factor * (branch_sum[:scen, columns] + branch_in[:, columns])
    for copy in homes:
        copy.wait()
    back = jnp.concatenate([state_out[...]] + [state_in[d - 1] for d in range(1, n)], 0)
    rank_row = jnp.sum(jnp.where(same & (rows_at < lanes_at), 1.0, 0.0), axis=0, keepdims=True)
    home = jnp.where(
        iota((cap, models), 0) == place * slots + rank_row.astype(jnp.int32), 1.0, 0.0
    ).astype(bf16)
    back = split_dot(back, home)
    out = jnp.zeros((scen, models), f32)
    for d in range(n):
        out = out + jnp.where(dest_row == (place + n - d) % n, back[d * scen : (d + 1) * scen], 0.0)
    current_ref[...] = out


def write_kernel(voltage_ref, current_ref, voltage_out, current_out, sems):
    copies = [
        pltpu.make_async_copy(voltage_ref, voltage_out, sems.at[0]),
        pltpu.make_async_copy(current_ref, current_out, sems.at[1]),
    ]
    for copy in copies:
        copy.start()
    for copy in copies:
        copy.wait()


def per_device(
    inverse,
    voltage_prev,
    line_delay,
    line_bus,
    line_impedance,
    line_past,
    model_dest,
    model_bus,
    model_gain,
    model_lag,
    model_state,
    model_source,
    switch_bus,
    switch_admittance,
):
    n = lax.axis_size("rows")
    groups = lax.axis_size("scen")
    local, width = inverse.shape
    scen = voltage_prev.shape[0]
    steps = model_source.shape[0]
    ends = line_bus.shape[1]
    models = model_bus.shape[0]
    depth_max = line_past.shape[0]
    slots = max(2, 2 * models // n)
    cap = n * slots
    f32, bf16 = jnp.float32, jnp.bfloat16
    subs = n // 2
    pad = max(128, 2 * ends)
    points = 2 * cap + pad
    cols = cap + pad
    wide = cols if pad > 2 * ends else cols + 128
    past_rows = depth_max * 2 * scen
    quarter = (16 + (steps + 1) * scen) // 4
    packed = pad == 128 and (subs - 1) * 2 * ends <= 128 and 4 * ends <= 128 and scen == 16
    line_rows = 8 if packed else scen
    copies = 3 * (n - 1) + (steps - 2) * (subs - 1) + 30
    vmem = pl.BlockSpec(memory_space=pltpu.VMEM)
    hbm = pl.BlockSpec(memory_space=pl.ANY)
    voltage, model_current = pl.pallas_call(
        functools.partial(step_kernel, n, steps, depth_max, cap, slots, pad, packed),
        out_shape=(pltpu.VMEM((scen, width), f32), pltpu.VMEM((scen, models), f32)),
        in_specs=[hbm] * 2 + [vmem] * 12,
        out_specs=(vmem, vmem),
        scratch_shapes=[
            pltpu.VMEM((local, width), bf16),
            pltpu.VMEM((scen, width), f32),
            pltpu.VMEM((8, pad), f32),
            pltpu.VMEM((8, pad), f32),
            pltpu.VMEM((past_rows, pad), f32),
            pltpu.VMEM((past_rows, pad), f32),
            pltpu.VMEM((8, 128), f32),
            pltpu.VMEM((groups - 1, 8, 128), f32),
            pltpu.VMEM((subs, 8, 256), f32),
            pltpu.VMEM((n, 8, 256), f32),
            pltpu.VMEM((subs, quarter, 256), f32),
            pltpu.VMEM((n, quarter, 256), f32),
            pltpu.VMEM((width, cols), bf16),
            pltpu.VMEM((cap + ends + groups * scen, local), bf16),
            pltpu.VMEM((cap + ends, width), bf16),
            pltpu.VMEM((cap // 2, width), bf16),
            pltpu.VMEM((ends, width // 2), bf16),
            pltpu.VMEM((points, width), bf16),
            pltpu.VMEM((points, points), bf16),
            pltpu.VMEM((groups * scen, width), f32),
            pltpu.VMEM((2 * scen, width), f32),
            pltpu.VMEM((2 * scen, width), f32),
            pltpu.VMEM((scen, width), f32),
            pltpu.VMEM((cap + ends, cols), bf16),
            pltpu.VMEM((cap + ends, cols), bf16),
            pltpu.VMEM((groups * scen, wide), f32),
            pltpu.VMEM((2 * scen, wide), f32),
            pltpu.VMEM((2 * scen, wide), f32),
            pltpu.VMEM((3, scen, wide), f32),
            pltpu.VMEM((scen, cap), f32),
            pltpu.VMEM((scen, cap), f32),
            pltpu.VMEM((4, cap, cap), bf16),
            pltpu.VMEM((4, ends, cols), bf16),
            pltpu.VMEM((points, points), bf16),
            pltpu.VMEM((steps - 2, subs - 1, line_rows, pad), f32),
            pltpu.VMEM((steps - 2, subs - 1, line_rows, pad), f32),
            pltpu.VMEM((scen, cap), f32),
            pltpu.VMEM((n - 1, scen, cap), f32),
            pltpu.SemaphoreType.DMA((2,)),
            pltpu.SemaphoreType.DMA((copies, 2)),
        ],
        compiler_params=pltpu.CompilerParams(
            collective_id=0, has_side_effects=True, vmem_limit_bytes=56 * 2**20
        ),
    )(
        inverse,
        voltage_prev,
        line_delay,
        line_bus,
        line_impedance,
        line_past.reshape(past_rows, ends),
        model_dest.reshape(1, models),
        model_bus.reshape(1, models),
        model_gain.reshape(1, models),
        model_lag.reshape(1, models),
        model_state,
        model_source.reshape(steps * scen, models),
        jnp.swapaxes(switch_bus, 1, 2),
        switch_admittance.T,
    )
    return pl.pallas_call(
        write_kernel,
        out_shape=(
            jax.ShapeDtypeStruct((scen, width), f32),
            jax.ShapeDtypeStruct((scen, models), f32),
        ),
        in_specs=[vmem, vmem],
        out_specs=(hbm, hbm),
        scratch_shapes=[pltpu.SemaphoreType.DMA((2,))],
    )(pltpu.with_memory_space_constraint(voltage, pltpu.VMEM), pltpu.with_memory_space_constraint(model_current, pltpu.VMEM))


def solution(mesh):
    placed = (
        P("scen", "rows"),
        P("scen", "rows"),
        P("rows", None),
        P("rows", None),
        P("rows", None),
        P(None, None, "scen", "rows", None),
        P("rows", None),
        P("rows"),
        P("rows"),
        P("rows"),
        P("scen", "rows"),
        P(None, "scen", "rows"),
        P(None, "scen", None),
        P("scen", None),
    )
    return jax.shard_map(
        per_device,
        mesh=mesh,
        in_specs=placed,
        out_specs=(P("scen", "rows"), P("scen", "rows")),
        check_vma=False,
    )
```

```python
import functools

import jax
import jax.numpy as jnp
from jax import lax
from jax.experimental import pallas as pl
from jax.experimental.pallas import tpu as pltpu
from jax.sharding import PartitionSpec as P


def split_dot(value, selector):
    rows = value.shape[0]
    high = value.astype(jnp.bfloat16)
    rest = value - high.astype(jnp.float32)
    middle = rest.astype(jnp.bfloat16)
    low = (rest - middle.astype(jnp.float32)).astype(jnp.bfloat16)
    stacked = jnp.concatenate([high, middle, low], 0)
    out = jnp.dot(stacked, selector, preferred_element_type=jnp.float32)
    return out[:rows] + out[rows : 2 * rows] + out[2 * rows :]


def bits(value):
    return value.bit_length() - 1


def step_kernel(
    n,
    steps,
    depth_max,
    cap,
    slots,
    pad,
    packed,
    tight,
    inverse_hbm,
    prev_hbm,
    delay_hbm,
    end_hbm,
    impedance_hbm,
    past_hbm,
    dest_hbm,
    bus_hbm,
    gain_hbm,
    lag_hbm,
    state_hbm,
    source_hbm,
    switch_hbm,
    admit_hbm,
    voltage_ref,
    current_ref,
    inverse_ref,
    prev_ref,
    delay_ref,
    end_ref,
    impedance_ref,
    past_ref,
    dest_ref,
    bus_ref,
    gain_ref,
    lag_ref,
    state_ref,
    source_ref,
    switch_ref,
    admit_ref,
    head_out,
    head_in,
    past_out,
    past_in,
    switch_out,
    switch_in,
    bus_out,
    bus_in,
    model_out,
    model_in,
    col_sel,
    row_sel,
    rows_part,
    rows_mate,
    ends_mate,
    solve,
    merge,
    branch_part,
    branch_mate,
    branch_sum,
    branch_in,
    part,
    part_in,
    side,
    side_mate,
    side_out,
    side_in,
    volt_out,
    volt_in,
    quads,
    line_rows,
    matrix,
    line_out,
    line_in,
    state_out,
    state_in,
    local_sems,
    sems,
):
    f32, bf16 = jnp.float32, jnp.bfloat16
    place = lax.axis_index("rows")
    share = lax.axis_index("scen")
    subs = n // 2
    subnet, half = place // 2, place % 2
    pair = place + 1 - 2 * half
    lower = half == 0
    top, core = share // 2, share % 2
    upward = top == 0
    mate, across, corner = share + 1 - 2 * core, (share + 2) % 4, 3 - share
    scen = state_ref.shape[0]
    local, width = inverse_ref.shape
    models = dest_ref.shape[1]
    ends = end_ref.shape[1]
    count = [0]

    def remote(src, dst, device):
        at = count[0]
        count[0] += 1
        return pltpu.make_async_remote_copy(
            src_ref=src,
            dst_ref=dst,
            send_sem=sems.at[at, 0],
            recv_sem=sems.at[at, 1],
            device_id=device,
            device_id_type=pl.DeviceIdType.MESH,
        )

    barrier = pltpu.get_barrier_semaphore()
    friends = [(place, mate), (place, across), (place, corner), (pair, across)]
    friends += [((place + d) % n, share) for d in range(1, n)]
    for device in friends:
        pl.semaphore_signal(barrier, inc=1, device_id=device, device_id_type=pl.DeviceIdType.MESH)
    arrays = [
        (dest_hbm, dest_ref),
        (bus_hbm, bus_ref),
        (switch_hbm, switch_ref),
        (admit_hbm, admit_ref),
        (delay_hbm, delay_ref),
        (end_hbm, end_ref),
        (impedance_hbm, impedance_ref),
        (past_hbm, past_ref),
        (lag_hbm, lag_ref),
        (gain_hbm, gain_ref),
        (state_hbm, state_ref),
        (source_hbm, source_ref),
        (inverse_hbm, inverse_ref),
        (prev_hbm, prev_ref),
    ]
    loads = [pltpu.make_async_copy(src, dst, local_sems.at[at]) for at, (src, dst) in enumerate(arrays)]
    for copy in loads:
        copy.start()
    load_inverse, load_prev = loads[12:]
    for copy in loads[:2]:
        copy.wait()

    iota = functools.partial(lax.broadcasted_iota, jnp.int32)
    group = 128 // slots
    dest_row = dest_ref[...]
    dest = jnp.broadcast_to(dest_row.astype(f32), (models, models))
    dest_col = dest.T
    same = dest == dest_col
    rows_at, lanes_at = iota((models, models), 0), iota((models, models), 1)
    rank_col = jnp.sum(jnp.where(same & (lanes_at < rows_at), 1.0, 0.0), axis=1, keepdims=True)
    dest_col = dest_col[:, 0:1].astype(jnp.int32)
    spot = (dest_col >> 1) * 256 + (dest_col & 1) * 128 + rank_col.astype(jnp.int32)
    spot = spot + (place % group) * slots
    placing = jnp.where(iota((models, subs * 256), 1) == spot, 1.0, 0.0).astype(bf16)
    bus_row = (bus_ref[...] + (dest_row & 1) * width + 1).astype(f32)
    spread = split_dot(jnp.broadcast_to(bus_row, (16, models)), placing)
    for g in range(subs):
        bus_out[g] = spread[:8, g * 256 : (g + 1) * 256]

    pl.semaphore_wait(barrier, len(friends))
    moved_buses = []
    for d in range(1, n):
        to = (place + d) % n
        moved_buses.append(remote(bus_out.at[to // 2], bus_in.at[place], (to, share)))
    for copy in moved_buses:
        copy.start()
    bus_in[place] = bus_out[subnet]
    for copy in loads[2:8]:
        copy.wait()
    switch_out[...] = jnp.zeros_like(switch_out)
    named = iota((subs, scen), 0) == subnet
    for row, values in enumerate((switch_ref[0].astype(f32), switch_ref[1].astype(f32), admit_ref[...])):
        switch_out[row : row + 1, :scen] = jnp.sum(jnp.where(named, values, 0.0), axis=0, keepdims=True)
    head_out[...] = jnp.zeros_like(head_out)
    head_out[0:1, :ends] = delay_ref[...].astype(f32)
    head_out[1:2, :ends] = impedance_ref[...]
    head_out[2:3, :ends] = (end_ref[...] + half * width + 1).astype(f32)
    head = head_out[...]
    head_out[...] = jnp.where(lower, head, pltpu.roll(head, ends, 1))
    past_out[...] = jnp.zeros_like(past_out)
    if packed:
        scale = 2.0 / jnp.where(delay_ref[...] == 0, 1.0, impedance_ref[...])
        for k in range(depth_max):
            older = past_ref[k * 2 * scen : (k + 1) * 2 * scen, :]
            past_out[:, k * 2 * ends : (2 * k + 1) * ends] = -scale * older[:scen] - older[scen:]
    else:
        past_out[:, :ends] = past_ref[...]
    past = past_out[...]
    past_out[...] = jnp.where(lower, past, pltpu.roll(past, ends, 1))

    switches = [
        remote(switch_out, switch_in.at[at], (place, to)) for at, to in enumerate((across, mate, corner))
    ]
    for copy in switches:
        copy.start()
    head_copy = remote(head_out, head_in, (pair, share))
    head_copy.start()
    past_copy = remote(past_out, past_in, (pair, share))
    past_copy.start()

    for copy in loads[8:12]:
        copy.wait()
    lag_row = lag_ref[...]
    gain_row = (1.0 - lag_row) * gain_ref[...]
    payload = jnp.concatenate(
        [
            jnp.broadcast_to(lag_row, (8, models)),
            jnp.broadcast_to(gain_row, (8, models)),
            state_ref[...],
            source_ref[...],
        ],
        0,
    )
    quarter = payload.shape[0] // 4
    for g in range(subs):
        base = split_dot(payload, placing[:, g * 256 : (g + 1) * 256])
        for h in range(2):
            lanes = slice(h * 128, (h + 1) * 128)
            total = base[:quarter, lanes]
            for q in range(1, 4):
                total = total + pltpu.roll(base[q * quarter : (q + 1) * quarter, lanes], 32 * q, 1)
            model_out[g, :, lanes] = total
    moved_models = []
    for d in range(1, n):
        to = (place + d) % n
        moved_models.append(remote(model_out.at[to // 2], model_in.at[place], (to, share)))
    for copy in moved_models:
        copy.start()
    model_in[place] = model_out[subnet]

    for copy in switches:
        copy.wait()
    switch = switch_out[...]
    for at in range(3):
        switch = switch + pltpu.roll(switch_in[at], scen * (at + 1), 1)
    switch = jnp.concatenate([switch] * 16, 0).T
    scens = 4 * scen
    pick_a, pick_b = switch[:scens, 0:1].astype(jnp.int32), switch[:scens, 1:2].astype(jnp.int32)
    admit = switch[:scen, 2:3]
    row_ids = iota((scens, local), 1) + share * local
    picks = (jnp.where(row_ids == pick_a, 1.0, 0.0) - jnp.where(row_ids == pick_b, 1.0, 0.0)).astype(bf16)
    load_inverse.wait()
    tile = min(width, 512)
    for at in range(0, width, tile):
        branch_part[:, at : at + tile] = jnp.dot(
            picks, inverse_ref[:, at : at + tile], preferred_element_type=f32
        )
    branch_copy = remote(branch_part.at[2 * scen :], branch_mate, (place, mate))
    branch_copy.start()

    head_copy.wait()
    for copy in moved_buses:
        copy.wait()
    head = head_out[...] + head_in[...]
    pieces = []
    for h in range(2):
        for g in range(n // group):
            total = bus_in[g * group, :, h * 128 : (h + 1) * 128]
            for k in range(1, group):
                total = total + bus_in[g * group + k, :, h * 128 : (h + 1) * 128]
            pieces.append(total)
    pts = jnp.concatenate(pieces + [jnp.broadcast_to(head[2:3], (8, pad))], 1)
    pts_col = pts.T[:, 0:1].astype(jnp.int32) - 1
    pts = pts[0:1].astype(jnp.int32) - 1
    points = 2 * cap + pad
    cols = cap + pad
    own_pts = jnp.concatenate(
        [jnp.where(lower, pts[:, :cap], pts[:, cap : 2 * cap]), pts[:, 2 * cap :]], 1
    ) - half * width
    minor = jnp.where(iota((128, cols), 0) == (own_pts & 127), 1.0, 0.0).astype(bf16)
    major = own_pts >> 7
    own_rows = jnp.concatenate(
        [
            jnp.where(upward, pts_col[:cap], pts_col[cap : 2 * cap]),
            jnp.where(upward, pts_col[2 * cap : 2 * cap + ends], pts_col[2 * cap + ends : 2 * cap + 2 * ends]),
        ],
        0,
    ) - share * local
    live = cap + ends
    row_sel[...] = jnp.where(iota((live, local), 1) == own_rows, 1.0, 0.0).astype(bf16)
    for at in range(0, width, tile):
        rows_part[:, at : at + tile] = jnp.dot(
            row_sel[...], inverse_ref[:, at : at + tile], preferred_element_type=f32
        ).astype(bf16)
        if at + tile == width // 2:
            branch_copy.wait()
            branch_sum[...] = branch_part[: 2 * scen] + branch_mate[...]
            branch_across = remote(branch_sum.at[scen:], branch_in, (place, across))
            branch_across.start()
        for row in range(at // 128, (at + tile) // 128):
            chosen = jnp.where(major == row, 1.0, 0.0).astype(bf16)
            col_sel[row * 128 : (row + 1) * 128] = minor * chosen
    part[...] = jnp.dot(rows_part[...], col_sel[...], preferred_element_type=f32).astype(bf16)
    part_copy = remote(part, part_in, (place, mate))
    part_copy.start()
    depth_part = jnp.zeros((scens, 1), f32)
    for at in range(0, width, tile):
        col_ids = iota((scens, tile), 1) + (half * width + at)
        signs = jnp.where(col_ids == pick_a, 1.0, 0.0) - jnp.where(col_ids == pick_b, 1.0, 0.0)
        depth_part = depth_part + jnp.sum(branch_part[:, at : at + tile] * signs, axis=1, keepdims=True)
    wide = side.shape[1]
    product = split_dot(branch_part[...], col_sel[...])
    if wide > cols:
        product = jnp.concatenate([product, jnp.zeros((scens, wide - cols), f32)], 1)
    side[...] = jnp.where(iota((scens, wide), 1) == wide - 1, depth_part, product)
    side_copy = remote(side.at[2 * scen :], side_mate, (place, mate))
    side_copy.start()
    load_prev.wait()
    volt_out[...] = split_dot(prev_ref[...], col_sel[:, :cap])
    volt_copy = remote(volt_out, volt_in, (pair, share))
    volt_copy.start()
    halfrows, halfwidth = cap // 2, width // 2
    own_half = pl.ds(pl.multiple_of(core * halfrows, 16), halfrows)
    mate_half = pl.ds(pl.multiple_of((1 - core) * halfrows, 16), halfrows)
    own_lanes = pl.ds(pl.multiple_of(core * halfwidth, 128), halfwidth)
    mate_lanes = pl.ds(pl.multiple_of((1 - core) * halfwidth, 128), halfwidth)
    rows_copy = remote(rows_part.at[mate_half], rows_mate, (place, mate))
    ends_copy = remote(rows_part.at[cap:, mate_lanes], ends_mate, (place, mate))

    mine = top * 2 + half
    part_copy.wait()
    whole = part[...] + part_in[...]
    quads[mine] = whole[:cap, :cap]
    line_rows[mine] = whole[cap:]
    others = [(pair, across), (place, across), (pair, share)]
    theirs = [(1 - top) * 2 + 1 - half, (1 - top) * 2 + half, top * 2 + 1 - half]
    quad_copies, row_copies, sides, forwards = [], [], [], []
    for device in others:
        row_copies.append(remote(line_rows.at[mine], line_rows.at[mine], device))
        row_copies[-1].start()
    side_copy.wait()
    side_out[...] = side[: 2 * scen] + side_mate[...]
    for at, device in enumerate(others):
        rows = slice(0, scen) if at == 2 else slice(scen, 2 * scen)
        sides.append(remote(side_out.at[rows], side_in.at[at], device))
        sides[-1].start()
    for device in others:
        quad_copies.append(remote(quads.at[mine, own_half], quads.at[mine, own_half], device))
        quad_copies[-1].start()
    rows_copy.start()
    ends_copy.start()
    equal = pts == pts_col
    sub_at = iota((points, points), 0)
    leader = jnp.min(jnp.where(equal, sub_at.astype(f32), float(points)), axis=0, keepdims=True)
    leading = leader == iota((1, points), 1).astype(f32)
    merge[...] = jnp.where(equal & leading, 1.0, 0.0).astype(bf16)
    lane = iota((1, pad), 1)
    per_pair = ends // n
    partner = (lane & (ends - 1)) >> bits(per_pair)
    origin = (partner & 1) * ends + (lane >> bits(ends)) * per_pair + (lane & (per_pair - 1))
    origin = jnp.where(lane < 2 * ends, origin + subnet * (2 * per_pair), -1)
    perm = jnp.where(iota((pad, pad), 0) == origin, 1.0, 0.0).astype(bf16)
    partner = partner >> 1
    if packed:
        way, spot = lane >> bits(2 * ends), lane & (2 * ends - 1)
        to = (subnet + way + 1) & (subs - 1)
        fellow = (spot & (ends - 1)) >> bits(per_pair)
        origin = (fellow & 1) * ends + (to * 2 + (spot >> bits(ends))) * per_pair + (spot & (per_pair - 1))
        sent = (way < subs - 1) & ((fellow >> 1) == subnet)
        spread = jnp.where(iota((pad, pad), 0) == jnp.where(sent, origin, -1), 1.0, 0.0).astype(bf16)

    rows_copy.wait()
    ends_copy.wait()
    if pad > 2 * ends:
        solve[2 * cap + 2 * ends :] = jnp.zeros((pad - 2 * ends, width), bf16)
    solve_rows = pl.ds(pl.multiple_of(top * cap + core * halfrows, 16), halfrows)
    solve_ends = pl.ds(pl.multiple_of(2 * cap + top * ends, 16), ends)
    solve[solve_rows] = rows_part[own_half] + rows_mate[...]
    solve[solve_ends, own_lanes] = rows_part[cap:, own_lanes] + ends_mate[...]
    their_ends = pl.ds(pl.multiple_of(2 * cap + (1 - top) * ends, 16), ends)
    spread_rows, spread_mate, spread_far = [], [], []
    chunk = halfrows // 4
    their_parts = []
    for at in range(4):
        first = pl.multiple_of(top * cap + core * halfrows + at * chunk, 16)
        there = solve.at[pl.ds(first, chunk)]
        spread_rows.append(remote(there, there, (place, across)))
        first = pl.multiple_of((1 - top) * cap + core * halfrows + at * chunk, 16)
        their_parts.append(solve.at[pl.ds(first, chunk)])
    there = solve.at[solve_ends, own_lanes]
    spread_rows.append(remote(there, there, (place, across)))
    their_parts.append(solve.at[their_ends, own_lanes])
    for there in (solve.at[solve_rows], solve.at[solve_ends, own_lanes]):
        spread_mate.append(remote(there, there, (place, mate)))

    def pass_on(parts):
        for at in parts:
            spread_rows[at].wait()
            spread_far.append(remote(their_parts[at], their_parts[at], (place, mate)))
            spread_far[-1].start()

    for copy in spread_rows:
        copy.start()

    for copy in sides:
        copy.wait()
    near = side_out[:scen] + side_in[1]
    far = side_in[0] + side_in[2]
    rest = near[:, cap:] + far[:, cap:]
    spare = iota((scen, pad), 1) < 2 * ends
    branch = jnp.concatenate(
        [
            jnp.where(lower, near[:, :cap], far[:, :cap]),
            jnp.where(lower, far[:, :cap], near[:, :cap]),
            jnp.where(spare, rest[:, :pad], 0.0),
        ],
        1,
    )
    depth = rest[:, wide - cap - 1 : wide - cap]
    volt_copy.wait()
    own_volt, other_volt = volt_out[...], volt_in[...]
    volt = jnp.concatenate(
        [jnp.where(lower, own_volt, other_volt), jnp.where(lower, other_volt, own_volt)], 1
    )
    delays, impedance = head[0:1], head[1:2]
    admittance = 2.0 / jnp.where(delays == 0.0, 1.0, impedance)
    past_copy.wait()
    past = past_out[...] + past_in[...]
    history = []
    for k in range(depth_max):
        if packed:
            history.append(pltpu.roll(past, (pad - k * 2 * ends) % pad, 1) if k else past)
        else:
            older = past[k * 2 * scen : (k + 1) * 2 * scen]
            history.append(-admittance * older[:scen] - older[scen:])
    branch_ends, admittance_ends = branch[:, 2 * cap :], admittance
    if packed:
        branch_ends = split_dot(branch_ends, spread)
        admittance_ends = split_dot(jnp.broadcast_to(admittance, (16, pad)), spread)[:1]
    for copy in moved_models:
        copy.wait()
    band_of = iota((quarter, 128), 1) >> 5
    received = [[] for _ in range(4)]
    for h in range(2):
        for g in range(n // group):
            bands = []
            for b in range(4):
                members = [g * group + k for k in range(group) if k * slots // 32 == b]
                total = model_in[members[0], :, h * 128 : (h + 1) * 128]
                for p in members[1:]:
                    total = total + model_in[p, :, h * 128 : (h + 1) * 128]
                bands.append(total)
            for q in range(4):
                total = bands[(3 - q) % 4]
                for b in range(3):
                    total = jnp.where(band_of == b, bands[(b - q) % 4], total)
                received[q].append(pltpu.roll(total, (128 - 32 * q) % 128, 1) if q else total)
    received = jnp.concatenate([jnp.concatenate(parts, 1) for parts in received], 0)
    lag, gain = received[0:1], received[8:9]
    current = received[16 : 16 + scen]
    lines = []
    homes = []
    for step in range(steps):
        current = lag * current + gain * (received[16 + (step + 1) * scen : 16 + (step + 2) * scen] - volt)
        if step + 1 == steps:
            mine = jnp.where(lower, current[:, :cap], current[:, cap:])
            if tight:
                for p in range(n):
                    block, shift = slice(p // 4 * 128, p // 4 * 128 + 128), p % 4 * 32
                    upper = pltpu.roll(mine[:8, block], 128 - shift, 1) if shift else mine[:8, block]
                    under = pltpu.roll(mine[8:, block], (192 - shift) % 128, 1) if shift != 64 else mine[8:, block]
                    state_out[p] = jnp.where(lane < 64, upper, under)
            else:
                state_out[0] = mine
            for d in range(1, n):
                to = (place + d) % n
                homes.append(
                    remote(state_out.at[to if tight else 0], state_in.at[place], (to, share))
                )
            for copy in homes:
                copy.start()
        feed = split_dot(current, merge[: 2 * cap])
        if step + 1 == steps:
            pass_on(range(3))
        if step >= 2:
            for copy in lines[step - 2]:
                copy.wait()
            arrived = line_in[step - 2, 0]
            if packed:
                for d in range(2, subs):
                    arrived = arrived + line_in[step - 2, d - 1]
                arrived = jnp.concatenate([arrived, pltpu.roll(arrived, pad // 2, 1)], 0)
            else:
                arrived = jnp.zeros((scen, pad), f32)
                for d in range(1, subs):
                    moved = split_dot(line_in[step - 2, d - 1], perm)
                    arrived = arrived + jnp.where(partner == (subnet + subs - d) % subs, moved, 0.0)
            history.append(arrived)
        line_term = jnp.zeros((scen, pad), f32)
        for delay in range(2, depth_max + 1):
            line_term = line_term + jnp.where(delays == delay, history[step - delay + depth_max], 0.0)
        feed = feed - split_dot(line_term, merge[2 * cap :])
        rhs = feed.astype(bf16)
        term_ends = split_dot(line_term, spread) if packed else line_term
        along = jnp.sum(rhs.astype(f32) * branch, axis=1, keepdims=True)
        factor = admit * along / (1.0 + admit * depth)
        if step == 0:
            for copy in row_copies:
                copy.wait()
            matrix[2 * cap :, :] = jnp.zeros((pad, points), bf16)
            for x in range(2):
                rows = slice(2 * cap + x * ends, 2 * cap + (x + 1) * ends)
                for h in range(2):
                    matrix[rows, h * cap : (h + 1) * cap] = line_rows[2 * x + h, :, :cap]
                matrix[rows, 2 * cap :] = line_rows[2 * x, :, cap:] + line_rows[2 * x + 1, :, cap:]
            matrix[: 2 * cap, 2 * cap :] = matrix[2 * cap :, : 2 * cap].astype(f32).T.astype(bf16)
            if packed:
                matrix[:, 2 * cap :] = jnp.dot(
                    matrix[:, 2 * cap :], spread, preferred_element_type=f32
                ).astype(bf16)
        if step + 2 < steps:
            sending = jnp.dot(rhs, matrix[:, 2 * cap :], preferred_element_type=f32)
            sending = -admittance_ends * (sending - factor * branch_ends) - term_ends
            for d in range(1, subs):
                if packed:
                    upper = pltpu.roll(sending[:8], (128 - 2 * ends * (d - 1)) % 128, 1) if d > 1 else sending[:8]
                    under = pltpu.roll(sending[8:], (64 - 2 * ends * (d - 1)) % 128, 1)
                    line_out[step, d - 1] = jnp.where(lane < 64, upper, under)
                else:
                    line_out[step, d - 1] = sending
            lines.append(
                [
                    remote(
                        line_out.at[step, d - 1],
                        line_in.at[step, d - 1],
                        (((subnet + d) % subs) * 2 + half, share),
                    )
                    for d in range(1, subs)
                ]
            )
            for copy in lines[step]:
                copy.start()
        if step == 0:
            for at in range(3):
                quad_copies[at].wait_recv()
                there = quads.at[theirs[at], own_half]
                forwards.append(remote(there, there, (place, mate)))
                forwards[-1].start()
            for copy in spread_mate:
                copy.start()
            for copy in quad_copies:
                copy.wait_send()
            for copy in forwards:
                copy.wait()
            for x in range(2):
                for h in range(2):
                    matrix[x * cap : (x + 1) * cap, h * cap : (h + 1) * cap] = quads[2 * x + h]
        if step + 1 < steps:
            volt = jnp.dot(rhs, matrix[:, : 2 * cap], preferred_element_type=f32)
            volt = volt - factor * branch[:, : 2 * cap]

    pass_on(range(3, 5))
    branch_across.wait()
    for copy in spread_mate + spread_far:
        copy.wait()
    for at in range(0, width, tile):
        columns = slice(at, at + tile)
        product = jnp.dot(rhs, solve[:, columns], preferred_element_type=f32)
        voltage_ref[:, columns] = product - factor * (branch_sum[:scen, columns] + branch_in[:, columns])
    for copy in homes:
        copy.wait()
    rank_row = jnp.sum(jnp.where(same & (rows_at < lanes_at), 1.0, 0.0), axis=0, keepdims=True)
    rank_row = rank_row.astype(jnp.int32)
    state_in[place] = state_out[place if tight else 0]
    if tight:
        blocks = []
        for g in range(n // 4):
            upper, under = state_in[4 * g], pltpu.roll(state_in[4 * g], 64, 1)
            for k in range(1, 4):
                tile_in = state_in[4 * g + k]
                upper = jnp.where(band_of[:8] == k, pltpu.roll(tile_in, 32 * k, 1), upper)
                under = jnp.where(
                    band_of[:8] == k, pltpu.roll(tile_in, (32 * k + 64) % 128, 1) if k != 2 else tile_in, under
                )
            blocks.append(jnp.concatenate([upper, under], 0))
        home = jnp.where(iota((cap, models), 0) == dest_row * slots + rank_row, 1.0, 0.0).astype(bf16)
        out = split_dot(jnp.concatenate(blocks, 1), home)
    else:
        home = jnp.where(iota((cap, models), 0) == place * slots + rank_row, 1.0, 0.0).astype(bf16)
        back = split_dot(jnp.concatenate([state_in[p] for p in range(n)], 0), home)
        out = jnp.zeros((scen, models), f32)
        for p in range(n):
            out = out + jnp.where(dest_row == p, back[p * scen : (p + 1) * scen], 0.0)
    current_ref[...] = out


def write_kernel(voltage_ref, current_ref, voltage_out, current_out, sems):
    copies = [
        pltpu.make_async_copy(voltage_ref, voltage_out, sems.at[0]),
        pltpu.make_async_copy(current_ref, current_out, sems.at[1]),
    ]
    for copy in copies:
        copy.start()
    for copy in copies:
        copy.wait()


def per_device(
    inverse,
    voltage_prev,
    line_delay,
    line_bus,
    line_impedance,
    line_past,
    model_dest,
    model_bus,
    model_gain,
    model_lag,
    model_state,
    model_source,
    switch_bus,
    switch_admittance,
):
    n = lax.axis_size("rows")
    groups = lax.axis_size("scen")
    local, width = inverse.shape
    scen = voltage_prev.shape[0]
    steps = model_source.shape[0]
    ends = line_bus.shape[1]
    models = model_bus.shape[0]
    depth_max = line_past.shape[0]
    slots = max(2, 2 * models // n)
    cap = n * slots
    f32, bf16 = jnp.float32, jnp.bfloat16
    subs = n // 2
    pad = max(128, 2 * ends)
    points = 2 * cap + pad
    cols = cap + pad
    wide = cols if pad > 2 * ends else cols + 128
    past_rows = depth_max * 2 * scen
    quarter = (16 + (steps + 1) * scen) // 4
    packed = pad == 128 and max(subs - 1, depth_max) * 2 * ends <= 128 and 4 * ends <= 128 and scen == 16
    line_rows = 8 if packed else scen
    tight = slots == 32 and n % 4 == 0 and scen == 16
    copies = 3 * (n - 1) + (steps - 2) * (subs - 1) + 36
    vmem = pl.BlockSpec(memory_space=pltpu.VMEM)
    hbm = pl.BlockSpec(memory_space=pl.ANY)
    voltage, model_current = pl.pallas_call(
        functools.partial(step_kernel, n, steps, depth_max, cap, slots, pad, packed, tight),
        out_shape=(pltpu.VMEM((scen, width), f32), pltpu.VMEM((scen, models), f32)),
        in_specs=[hbm] * 14,
        out_specs=(vmem, vmem),
        scratch_shapes=[
            pltpu.VMEM((local, width), bf16),
            pltpu.VMEM((scen, width), f32),
            pltpu.VMEM((1, ends), jnp.int32),
            pltpu.VMEM((1, ends), jnp.int32),
            pltpu.VMEM((1, ends), f32),
            pltpu.VMEM((past_rows, ends), f32),
            pltpu.VMEM((1, models), jnp.int32),
            pltpu.VMEM((1, models), jnp.int32),
            pltpu.VMEM((1, models), f32),
            pltpu.VMEM((1, models), f32),
            pltpu.VMEM((scen, models), f32),
            pltpu.VMEM((steps * scen, models), f32),
            pltpu.VMEM((2, subs, scen), jnp.int32),
            pltpu.VMEM((subs, scen), f32),
            pltpu.VMEM((8, pad), f32),
            pltpu.VMEM((8, pad), f32),
            pltpu.VMEM((scen if packed else past_rows, pad), f32),
            pltpu.VMEM((scen if packed else past_rows, pad), f32),
            pltpu.VMEM((8, 128), f32),
            pltpu.VMEM((groups - 1, 8, 128), f32),
            pltpu.VMEM((subs, 8, 256), f32),
            pltpu.VMEM((n, 8, 256), f32),
            pltpu.VMEM((subs, quarter, 256), f32),
            pltpu.VMEM((n, quarter, 256), f32),
            pltpu.VMEM((width, cols), bf16),
            pltpu.VMEM((cap + ends, local), bf16),
            pltpu.VMEM((cap + ends, width), bf16),
            pltpu.VMEM((cap // 2, width), bf16),
            pltpu.VMEM((ends, width // 2), bf16),
            pltpu.VMEM((points, width), bf16),
            pltpu.VMEM((points, points), bf16),
            pltpu.VMEM((groups * scen, width), f32),
            pltpu.VMEM((2 * scen, width), f32),
            pltpu.VMEM((2 * scen, width), f32),
            pltpu.VMEM((scen, width), f32),
            pltpu.VMEM((cap + ends, cols), bf16),
            pltpu.VMEM((cap + ends, cols), bf16),
            pltpu.VMEM((groups * scen, wide), f32),
            pltpu.VMEM((2 * scen, wide), f32),
            pltpu.VMEM((2 * scen, wide), f32),
            pltpu.VMEM((3, scen, wide), f32),
            pltpu.VMEM((scen, cap), f32),
            pltpu.VMEM((scen, cap), f32),
            pltpu.VMEM((4, cap, cap), bf16),
            pltpu.VMEM((4, ends, cols), bf16),
            pltpu.VMEM((points, points), bf16),
            pltpu.VMEM((steps - 2, subs - 1, line_rows, pad), f32),
            pltpu.VMEM((steps - 2, subs - 1, line_rows, pad), f32),
            pltpu.VMEM((n, 8, 128) if tight else (1, scen, cap), f32),
            pltpu.VMEM((n, 8, 128) if tight else (n, scen, cap), f32),
            pltpu.SemaphoreType.DMA((14,)),
            pltpu.SemaphoreType.DMA((copies, 2)),
        ],
        compiler_params=pltpu.CompilerParams(
            collective_id=0, has_side_effects=True, vmem_limit_bytes=56 * 2**20
        ),
    )(
        inverse,
        voltage_prev,
        line_delay,
        line_bus,
        line_impedance,
        line_past.reshape(past_rows, ends),
        model_dest.reshape(1, models),
        model_bus.reshape(1, models),
        model_gain.reshape(1, models),
        model_lag.reshape(1, models),
        model_state,
        model_source.reshape(steps * scen, models),
        jnp.swapaxes(switch_bus, 1, 2),
        switch_admittance.T,
    )
    return pl.pallas_call(
        write_kernel,
        out_shape=(
            jax.ShapeDtypeStruct((scen, width), f32),
            jax.ShapeDtypeStruct((scen, models), f32),
        ),
        in_specs=[vmem, vmem],
        out_specs=(hbm, hbm),
        scratch_shapes=[pltpu.SemaphoreType.DMA((2,))],
    )(pltpu.with_memory_space_constraint(voltage, pltpu.VMEM), pltpu.with_memory_space_constraint(model_current, pltpu.VMEM))


def solution(mesh):
    placed = (
        P("scen", "rows"),
        P("scen", "rows"),
        P("rows", None),
        P("rows", None),
        P("rows", None),
        P(None, None, "scen", "rows", None),
        P("rows", None),
        P("rows"),
        P("rows"),
        P("rows"),
        P("scen", "rows"),
        P(None, "scen", "rows"),
        P(None, "scen", None),
        P("scen", None),
    )
    return jax.shard_map(
        per_device,
        mesh=mesh,
        in_specs=placed,
        out_specs=(P("scen", "rows"), P("scen", "rows")),
        check_vma=False,
    )
```

```python
import functools

import jax
import jax.numpy as jnp
from jax import lax
from jax.experimental import pallas as pl
from jax.experimental.pallas import tpu as pltpu
from jax.sharding import PartitionSpec as P


def split_dot(value, selector):
    rows = value.shape[0]
    high = value.astype(jnp.bfloat16)
    rest = value - high.astype(jnp.float32)
    middle = rest.astype(jnp.bfloat16)
    low = (rest - middle.astype(jnp.float32)).astype(jnp.bfloat16)
    stacked = jnp.concatenate([high, middle, low], 0)
    out = jnp.dot(stacked, selector, preferred_element_type=jnp.float32)
    return out[:rows] + out[rows : 2 * rows] + out[2 * rows :]


def bits(value):
    return value.bit_length() - 1


def step_kernel(
    n,
    steps,
    depth_max,
    cap,
    slots,
    pad,
    packed,
    tight,
    inverse_hbm,
    prev_hbm,
    delay_hbm,
    end_hbm,
    impedance_hbm,
    past_hbm,
    dest_hbm,
    bus_hbm,
    gain_hbm,
    lag_hbm,
    state_hbm,
    source_hbm,
    switch_hbm,
    admit_hbm,
    voltage_ref,
    current_ref,
    inverse_ref,
    prev_ref,
    delay_ref,
    end_ref,
    impedance_ref,
    past_ref,
    dest_ref,
    bus_ref,
    gain_ref,
    lag_ref,
    state_ref,
    source_ref,
    switch_ref,
    admit_ref,
    head_out,
    head_in,
    past_out,
    past_in,
    switch_out,
    switch_in,
    bus_out,
    bus_in,
    model_out,
    model_in,
    col_sel,
    row_sel,
    rows_part,
    rows_mate,
    ends_mate,
    solve,
    merge,
    branch_part,
    branch_mate,
    branch_sum,
    branch_in,
    part,
    part_in,
    side,
    side_mate,
    side_out,
    side_in,
    volt_out,
    volt_in,
    quads,
    line_rows,
    matrix,
    line_out,
    line_in,
    state_out,
    state_in,
    local_sems,
    sems,
):
    f32, bf16 = jnp.float32, jnp.bfloat16
    place = lax.axis_index("rows")
    share = lax.axis_index("scen")
    subs = n // 2
    subnet, half = place // 2, place % 2
    pair = place + 1 - 2 * half
    lower = half == 0
    top, core = share // 2, share % 2
    upward = top == 0
    mate, across, corner = share + 1 - 2 * core, (share + 2) % 4, 3 - share
    scen = state_ref.shape[0]
    local, width = inverse_ref.shape
    models = dest_ref.shape[1]
    ends = end_ref.shape[1]
    count = [0]

    def remote(src, dst, device):
        at = count[0]
        count[0] += 1
        return pltpu.make_async_remote_copy(
            src_ref=src,
            dst_ref=dst,
            send_sem=sems.at[at, 0],
            recv_sem=sems.at[at, 1],
            device_id=device,
            device_id_type=pl.DeviceIdType.MESH,
        )

    barrier = pltpu.get_barrier_semaphore()
    friends = [(place, mate), (place, across), (place, corner), (pair, across)]
    friends += [((place + d) % n, share) for d in range(1, n)]
    for device in friends:
        pl.semaphore_signal(barrier, inc=1, device_id=device, device_id_type=pl.DeviceIdType.MESH)
    arrays = [
        (dest_hbm, dest_ref),
        (bus_hbm, bus_ref),
        (switch_hbm, switch_ref),
        (admit_hbm, admit_ref),
        (delay_hbm, delay_ref),
        (end_hbm, end_ref),
        (impedance_hbm, impedance_ref),
        (past_hbm, past_ref),
        (lag_hbm, lag_ref),
        (gain_hbm, gain_ref),
        (state_hbm, state_ref),
        (source_hbm, source_ref),
        (inverse_hbm, inverse_ref),
        (prev_hbm, prev_ref),
    ]
    loads = [pltpu.make_async_copy(src, dst, local_sems.at[at]) for at, (src, dst) in enumerate(arrays)]
    for copy in loads:
        copy.start()
    load_inverse, load_prev = loads[12:]
    for copy in loads[:2]:
        copy.wait()

    iota = functools.partial(lax.broadcasted_iota, jnp.int32)
    group = 128 // slots
    dest_row = dest_ref[...]
    dest = jnp.broadcast_to(dest_row.astype(f32), (models, models))
    dest_col = dest.T
    same = dest == dest_col
    rows_at, lanes_at = iota((models, models), 0), iota((models, models), 1)
    rank_col = jnp.sum(jnp.where(same & (lanes_at < rows_at), 1.0, 0.0), axis=1, keepdims=True)
    dest_col = dest_col[:, 0:1].astype(jnp.int32)
    spot = (dest_col >> 1) * 256 + (dest_col & 1) * 128 + rank_col.astype(jnp.int32)
    spot = spot + (place % group) * slots
    placing = jnp.where(iota((models, subs * 256), 1) == spot, 1.0, 0.0).astype(bf16)
    bus_row = (bus_ref[...] + (dest_row & 1) * width + 1).astype(f32)
    spread = split_dot(jnp.broadcast_to(bus_row, (16, models)), placing)
    for g in range(subs):
        bus_out[g] = spread[:8, g * 256 : (g + 1) * 256]

    pl.semaphore_wait(barrier, len(friends))
    moved_buses = []
    for d in range(1, n):
        to = (place + d) % n
        moved_buses.append(remote(bus_out.at[to // 2], bus_in.at[place], (to, share)))
    for copy in moved_buses:
        copy.start()
    bus_in[place] = bus_out[subnet]
    for copy in loads[2:8]:
        copy.wait()
    switch_out[...] = jnp.zeros_like(switch_out)
    named = iota((subs, scen), 0) == subnet
    for row, values in enumerate((switch_ref[0].astype(f32), switch_ref[1].astype(f32), admit_ref[...])):
        switch_out[row : row + 1, :scen] = jnp.sum(jnp.where(named, values, 0.0), axis=0, keepdims=True)
    head_out[...] = jnp.zeros_like(head_out)
    head_out[0:1, :ends] = delay_ref[...].astype(f32)
    head_out[1:2, :ends] = impedance_ref[...]
    head_out[2:3, :ends] = (end_ref[...] + half * width + 1).astype(f32)
    head = head_out[...]
    head_out[...] = jnp.where(lower, head, pltpu.roll(head, ends, 1))
    past_out[...] = jnp.zeros_like(past_out)
    if packed:
        scale = 2.0 / jnp.where(delay_ref[...] == 0, 1.0, impedance_ref[...])
        for k in range(depth_max):
            older = past_ref[k * 2 * scen : (k + 1) * 2 * scen, :]
            past_out[:, k * 2 * ends : (2 * k + 1) * ends] = -scale * older[:scen] - older[scen:]
    else:
        past_out[:, :ends] = past_ref[...]
    past = past_out[...]
    past_out[...] = jnp.where(lower, past, pltpu.roll(past, ends, 1))

    switches = [
        remote(switch_out, switch_in.at[at], (place, to)) for at, to in enumerate((across, mate, corner))
    ]
    for copy in switches:
        copy.start()
    head_copy = remote(head_out, head_in, (pair, share))
    head_copy.start()
    past_copy = remote(past_out, past_in, (pair, share))
    past_copy.start()

    for copy in loads[8:12]:
        copy.wait()
    lag_row = lag_ref[...]
    gain_row = (1.0 - lag_row) * gain_ref[...]
    payload = jnp.concatenate(
        [
            jnp.broadcast_to(lag_row, (8, models)),
            jnp.broadcast_to(gain_row, (8, models)),
            state_ref[...],
            source_ref[...],
        ],
        0,
    )
    quarter = payload.shape[0] // 4
    for g in range(subs):
        base = split_dot(payload, placing[:, g * 256 : (g + 1) * 256])
        for h in range(2):
            lanes = slice(h * 128, (h + 1) * 128)
            total = base[:quarter, lanes]
            for q in range(1, 4):
                total = total + pltpu.roll(base[q * quarter : (q + 1) * quarter, lanes], 32 * q, 1)
            model_out[g, :, lanes] = total
    moved_models = []
    for d in range(1, n):
        to = (place + d) % n
        moved_models.append(remote(model_out.at[to // 2], model_in.at[place], (to, share)))
    for copy in moved_models:
        copy.start()
    model_in[place] = model_out[subnet]

    for copy in switches:
        copy.wait()
    switch = switch_out[...]
    for at in range(3):
        switch = switch + pltpu.roll(switch_in[at], scen * (at + 1), 1)
    switch = jnp.concatenate([switch] * 16, 0).T
    scens = 4 * scen
    pick_a, pick_b = switch[:scens, 0:1].astype(jnp.int32), switch[:scens, 1:2].astype(jnp.int32)
    admit = switch[:scen, 2:3]
    row_ids = iota((scens, local), 1) + share * local
    picks = (jnp.where(row_ids == pick_a, 1.0, 0.0) - jnp.where(row_ids == pick_b, 1.0, 0.0)).astype(bf16)
    load_inverse.wait()
    tile = min(width, 512)
    for at in range(0, width, tile):
        branch_part[:, at : at + tile] = jnp.dot(
            picks, inverse_ref[:, at : at + tile], preferred_element_type=f32
        )
    branch_copy = remote(branch_part.at[2 * scen :], branch_mate, (place, mate))
    branch_copy.start()

    head_copy.wait()
    for copy in moved_buses:
        copy.wait()
    head = head_out[...] + head_in[...]
    pieces = []
    for h in range(2):
        for g in range(n // group):
            total = bus_in[g * group, :, h * 128 : (h + 1) * 128]
            for k in range(1, group):
                total = total + bus_in[g * group + k, :, h * 128 : (h + 1) * 128]
            pieces.append(total)
    pts = jnp.concatenate(pieces + [jnp.broadcast_to(head[2:3], (8, pad))], 1)
    pts_col = pts.T[:, 0:1].astype(jnp.int32) - 1
    pts = pts[0:1].astype(jnp.int32) - 1
    points = 2 * cap + pad
    cols = cap + pad
    own_pts = jnp.concatenate(
        [jnp.where(lower, pts[:, :cap], pts[:, cap : 2 * cap]), pts[:, 2 * cap :]], 1
    ) - half * width
    minor = jnp.where(iota((128, cols), 0) == (own_pts & 127), 1.0, 0.0).astype(bf16)
    major = own_pts >> 7
    own_rows = jnp.concatenate(
        [
            jnp.where(upward, pts_col[:cap], pts_col[cap : 2 * cap]),
            jnp.where(upward, pts_col[2 * cap : 2 * cap + ends], pts_col[2 * cap + ends : 2 * cap + 2 * ends]),
        ],
        0,
    ) - share * local
    live = cap + ends
    row_sel[...] = jnp.where(iota((live, local), 1) == own_rows, 1.0, 0.0).astype(bf16)
    for at in range(0, width, tile):
        rows_part[:, at : at + tile] = jnp.dot(
            row_sel[...], inverse_ref[:, at : at + tile], preferred_element_type=f32
        ).astype(bf16)
        if at + tile == width // 2:
            branch_copy.wait()
            branch_sum[...] = branch_part[: 2 * scen] + branch_mate[...]
            branch_across = remote(branch_sum.at[scen:], branch_in, (place, across))
            branch_across.start()
        for row in range(at // 128, (at + tile) // 128):
            chosen = jnp.where(major == row, 1.0, 0.0).astype(bf16)
            col_sel[row * 128 : (row + 1) * 128] = minor * chosen
    part[...] = jnp.dot(rows_part[...], col_sel[...], preferred_element_type=f32).astype(bf16)
    part_copy = remote(part, part_in, (place, mate))
    part_copy.start()
    depth_part = jnp.zeros((scens, 1), f32)
    for at in range(0, width, tile):
        col_ids = iota((scens, tile), 1) + (half * width + at)
        signs = jnp.where(col_ids == pick_a, 1.0, 0.0) - jnp.where(col_ids == pick_b, 1.0, 0.0)
        depth_part = depth_part + jnp.sum(branch_part[:, at : at + tile] * signs, axis=1, keepdims=True)
    wide = side.shape[1]
    product = split_dot(branch_part[...], col_sel[...])
    if wide > cols:
        product = jnp.concatenate([product, jnp.zeros((scens, wide - cols), f32)], 1)
    side[...] = jnp.where(iota((scens, wide), 1) == wide - 1, depth_part, product)
    side_copy = remote(side.at[2 * scen :], side_mate, (place, mate))
    side_copy.start()
    load_prev.wait()
    volt_out[...] = split_dot(prev_ref[...], col_sel[:, :cap])
    volt_copy = remote(volt_out, volt_in, (pair, share))
    volt_copy.start()
    halfrows, halfwidth = cap // 2, width // 2
    own_half = pl.ds(pl.multiple_of(core * halfrows, 16), halfrows)
    mate_half = pl.ds(pl.multiple_of((1 - core) * halfrows, 16), halfrows)
    own_lanes = pl.ds(pl.multiple_of(core * halfwidth, 128), halfwidth)
    mate_lanes = pl.ds(pl.multiple_of((1 - core) * halfwidth, 128), halfwidth)
    rows_copy = remote(rows_part.at[mate_half], rows_mate, (place, mate))
    ends_copy = remote(rows_part.at[cap:, mate_lanes], ends_mate, (place, mate))
    rows_copy.start()
    ends_copy.start()

    mine = top * 2 + half
    part_copy.wait()
    whole = part[...] + part_in[...]
    quads[mine] = whole[:cap, :cap]
    line_rows[mine] = whole[cap:]
    others = [(pair, across), (place, across), (pair, share)]
    theirs = [(1 - top) * 2 + 1 - half, (1 - top) * 2 + half, top * 2 + 1 - half]
    quad_copies, row_copies, sides, forwards = [], [], [], []
    for device in others:
        row_copies.append(remote(line_rows.at[mine], line_rows.at[mine], device))
        row_copies[-1].start()
    side_copy.wait()
    side_out[...] = side[: 2 * scen] + side_mate[...]
    for at, device in enumerate(others):
        rows = slice(0, scen) if at == 2 else slice(scen, 2 * scen)
        sides.append(remote(side_out.at[rows], side_in.at[at], device))
        sides[-1].start()
    for device in others:
        quad_copies.append(remote(quads.at[mine, own_half], quads.at[mine, own_half], device))
        quad_copies[-1].start()
    rows_copy.wait()
    ends_copy.wait()
    if pad > 2 * ends:
        solve[2 * cap + 2 * ends :] = jnp.zeros((pad - 2 * ends, width), bf16)
    solve_rows = pl.ds(pl.multiple_of(top * cap + core * halfrows, 16), halfrows)
    solve_ends = pl.ds(pl.multiple_of(2 * cap + top * ends, 16), ends)
    solve[solve_rows] = rows_part[own_half] + rows_mate[...]
    solve[solve_ends, own_lanes] = rows_part[cap:, own_lanes] + ends_mate[...]
    their_ends = pl.ds(pl.multiple_of(2 * cap + (1 - top) * ends, 16), ends)
    spread_rows, spread_mate, spread_far = [], [], []
    chunk = halfrows // 4
    their_parts = []
    there = solve.at[solve_ends, own_lanes]
    spread_rows.append(remote(there, there, (place, across)))
    their_parts.append(solve.at[their_ends, own_lanes])
    for at in range(4):
        first = pl.multiple_of(top * cap + core * halfrows + at * chunk, 16)
        there = solve.at[pl.ds(first, chunk)]
        spread_rows.append(remote(there, there, (place, across)))
        first = pl.multiple_of((1 - top) * cap + core * halfrows + at * chunk, 16)
        their_parts.append(solve.at[pl.ds(first, chunk)])
    for there in (solve.at[solve_rows], solve.at[solve_ends, own_lanes]):
        spread_mate.append(remote(there, there, (place, mate)))

    def pass_on(parts):
        for at in parts:
            spread_rows[at].wait()
            spread_far.append(remote(their_parts[at], their_parts[at], (place, mate)))
            spread_far[-1].start()

    for copy in spread_rows:
        copy.start()
    equal = pts == pts_col
    sub_at = iota((points, points), 0)
    leader = jnp.min(jnp.where(equal, sub_at.astype(f32), float(points)), axis=0, keepdims=True)
    leading = leader == iota((1, points), 1).astype(f32)
    merge[...] = jnp.where(equal & leading, 1.0, 0.0).astype(bf16)
    lane = iota((1, pad), 1)
    per_pair = ends // n
    partner = (lane & (ends - 1)) >> bits(per_pair)
    origin = (partner & 1) * ends + (lane >> bits(ends)) * per_pair + (lane & (per_pair - 1))
    origin = jnp.where(lane < 2 * ends, origin + subnet * (2 * per_pair), -1)
    perm = jnp.where(iota((pad, pad), 0) == origin, 1.0, 0.0).astype(bf16)
    partner = partner >> 1
    if packed:
        way, spot = lane >> bits(2 * ends), lane & (2 * ends - 1)
        to = (subnet + way + 1) & (subs - 1)
        fellow = (spot & (ends - 1)) >> bits(per_pair)
        origin = (fellow & 1) * ends + (to * 2 + (spot >> bits(ends))) * per_pair + (spot & (per_pair - 1))
        sent = (way < subs - 1) & ((fellow >> 1) == subnet)
        spread = jnp.where(iota((pad, pad), 0) == jnp.where(sent, origin, -1), 1.0, 0.0).astype(bf16)


    for copy in sides:
        copy.wait()
    near = side_out[:scen] + side_in[1]
    far = side_in[0] + side_in[2]
    rest = near[:, cap:] + far[:, cap:]
    spare = iota((scen, pad), 1) < 2 * ends
    branch = jnp.concatenate(
        [
            jnp.where(lower, near[:, :cap], far[:, :cap]),
            jnp.where(lower, far[:, :cap], near[:, :cap]),
            jnp.where(spare, rest[:, :pad], 0.0),
        ],
        1,
    )
    depth = rest[:, wide - cap - 1 : wide - cap]
    volt_copy.wait()
    own_volt, other_volt = volt_out[...], volt_in[...]
    volt = jnp.concatenate(
        [jnp.where(lower, own_volt, other_volt), jnp.where(lower, other_volt, own_volt)], 1
    )
    delays, impedance = head[0:1], head[1:2]
    admittance = 2.0 / jnp.where(delays == 0.0, 1.0, impedance)
    past_copy.wait()
    past = past_out[...] + past_in[...]
    history = []
    for k in range(depth_max):
        if packed:
            history.append(pltpu.roll(past, (pad - k * 2 * ends) % pad, 1) if k else past)
        else:
            older = past[k * 2 * scen : (k + 1) * 2 * scen]
            history.append(-admittance * older[:scen] - older[scen:])
    branch_ends, admittance_ends = branch[:, 2 * cap :], admittance
    if packed:
        branch_ends = split_dot(branch_ends, spread)
        admittance_ends = split_dot(jnp.broadcast_to(admittance, (16, pad)), spread)[:1]
    for copy in moved_models:
        copy.wait()
    band_of = iota((quarter, 128), 1) >> 5
    received = [[] for _ in range(4)]
    for h in range(2):
        for g in range(n // group):
            bands = []
            for b in range(4):
                members = [g * group + k for k in range(group) if k * slots // 32 == b]
                total = model_in[members[0], :, h * 128 : (h + 1) * 128]
                for p in members[1:]:
                    total = total + model_in[p, :, h * 128 : (h + 1) * 128]
                bands.append(total)
            for q in range(4):
                total = bands[(3 - q) % 4]
                for b in range(3):
                    total = jnp.where(band_of == b, bands[(b - q) % 4], total)
                received[q].append(pltpu.roll(total, (128 - 32 * q) % 128, 1) if q else total)
    received = jnp.concatenate([jnp.concatenate(parts, 1) for parts in received], 0)
    lag, gain = received[0:1], received[8:9]
    current = received[16 : 16 + scen]
    lines = []
    homes = []
    for step in range(steps):
        current = lag * current + gain * (received[16 + (step + 1) * scen : 16 + (step + 2) * scen] - volt)
        if step + 1 == steps:
            mine = jnp.where(lower, current[:, :cap], current[:, cap:])
            if tight:
                for p in range(n):
                    block, shift = slice(p // 4 * 128, p // 4 * 128 + 128), p % 4 * 32
                    upper = pltpu.roll(mine[:8, block], 128 - shift, 1) if shift else mine[:8, block]
                    under = pltpu.roll(mine[8:, block], (192 - shift) % 128, 1) if shift != 64 else mine[8:, block]
                    state_out[p] = jnp.where(lane < 64, upper, under)
            else:
                state_out[0] = mine
            for d in range(1, n):
                to = (place + d) % n
                homes.append(
                    remote(state_out.at[to if tight else 0], state_in.at[place], (to, share))
                )
            for copy in homes:
                copy.start()
        feed = split_dot(current, merge[: 2 * cap])
        if step + 1 == steps:
            pass_on(range(3))
        if step >= 2:
            for copy in lines[step - 2]:
                copy.wait()
            arrived = line_in[step - 2, 0]
            if packed:
                for d in range(2, subs):
                    arrived = arrived + line_in[step - 2, d - 1]
                arrived = jnp.concatenate([arrived, pltpu.roll(arrived, pad // 2, 1)], 0)
            else:
                arrived = jnp.zeros((scen, pad), f32)
                for d in range(1, subs):
                    moved = split_dot(line_in[step - 2, d - 1], perm)
                    arrived = arrived + jnp.where(partner == (subnet + subs - d) % subs, moved, 0.0)
            history.append(arrived)
        line_term = jnp.zeros((scen, pad), f32)
        for delay in range(2, depth_max + 1):
            line_term = line_term + jnp.where(delays == delay, history[step - delay + depth_max], 0.0)
        feed = feed - split_dot(line_term, merge[2 * cap :])
        rhs = feed.astype(bf16)
        term_ends = split_dot(line_term, spread) if packed else line_term
        along = jnp.sum(rhs.astype(f32) * branch, axis=1, keepdims=True)
        factor = admit * along / (1.0 + admit * depth)
        if step == 0:
            for copy in row_copies:
                copy.wait()
            matrix[2 * cap :, :] = jnp.zeros((pad, points), bf16)
            for x in range(2):
                rows = slice(2 * cap + x * ends, 2 * cap + (x + 1) * ends)
                for h in range(2):
                    matrix[rows, h * cap : (h + 1) * cap] = line_rows[2 * x + h, :, :cap]
                matrix[rows, 2 * cap :] = line_rows[2 * x, :, cap:] + line_rows[2 * x + 1, :, cap:]
            matrix[: 2 * cap, 2 * cap :] = matrix[2 * cap :, : 2 * cap].astype(f32).T.astype(bf16)
            if packed:
                matrix[:, 2 * cap :] = jnp.dot(
                    matrix[:, 2 * cap :], spread, preferred_element_type=f32
                ).astype(bf16)
        if step + 2 < steps:
            sending = jnp.dot(rhs, matrix[:, 2 * cap :], preferred_element_type=f32)
            sending = -admittance_ends * (sending - factor * branch_ends) - term_ends
            for d in range(1, subs):
                if packed:
                    upper = pltpu.roll(sending[:8], (128 - 2 * ends * (d - 1)) % 128, 1) if d > 1 else sending[:8]
                    under = pltpu.roll(sending[8:], (64 - 2 * ends * (d - 1)) % 128, 1)
                    line_out[step, d - 1] = jnp.where(lane < 64, upper, under)
                else:
                    line_out[step, d - 1] = sending
            lines.append(
                [
                    remote(
                        line_out.at[step, d - 1],
                        line_in.at[step, d - 1],
                        (((subnet + d) % subs) * 2 + half, share),
                    )
                    for d in range(1, subs)
                ]
            )
            for copy in lines[step]:
                copy.start()
        if step == 0:
            for at in range(3):
                quad_copies[at].wait_recv()
                there = quads.at[theirs[at], own_half]
                forwards.append(remote(there, there, (place, mate)))
                forwards[-1].start()
            for copy in spread_mate:
                copy.start()
            for copy in quad_copies:
                copy.wait_send()
            for copy in forwards:
                copy.wait()
            for x in range(2):
                for h in range(2):
                    matrix[x * cap : (x + 1) * cap, h * cap : (h + 1) * cap] = quads[2 * x + h]
        if step + 1 < steps:
            volt = jnp.dot(rhs, matrix[:, : 2 * cap], preferred_element_type=f32)
            volt = volt - factor * branch[:, : 2 * cap]

    pass_on([3])
    branch_across.wait()
    for copy in spread_mate + spread_far[:1]:
        copy.wait()
    near = jnp.concatenate([jnp.where(upward, rhs[:, :cap], rhs[:, cap : 2 * cap]), rhs[:, 2 * cap :]], 1)
    far = jnp.where(upward, rhs[:, cap : 2 * cap], rhs[:, :cap])
    near_rows = pl.ds(pl.multiple_of(top * cap, 16), cap)
    for at in range(0, width, tile):
        columns = slice(at, at + tile)
        product = jnp.dot(near[:, :cap], solve[near_rows, columns], preferred_element_type=f32)
        product = product + jnp.dot(near[:, cap:], solve[2 * cap :, columns], preferred_element_type=f32)
        voltage_ref[:, columns] = product - factor * (branch_sum[:scen, columns] + branch_in[:, columns])
    for copy in homes:
        copy.wait()
    rank_row = jnp.sum(jnp.where(same & (rows_at < lanes_at), 1.0, 0.0), axis=0, keepdims=True)
    rank_row = rank_row.astype(jnp.int32)
    state_in[place] = state_out[place if tight else 0]
    if tight:
        blocks = []
        for g in range(n // 4):
            upper, under = state_in[4 * g], pltpu.roll(state_in[4 * g], 64, 1)
            for k in range(1, 4):
                tile_in = state_in[4 * g + k]
                upper = jnp.where(band_of[:8] == k, pltpu.roll(tile_in, 32 * k, 1), upper)
                under = jnp.where(
                    band_of[:8] == k, pltpu.roll(tile_in, (32 * k + 64) % 128, 1) if k != 2 else tile_in, under
                )
            blocks.append(jnp.concatenate([upper, under], 0))
        home = jnp.where(iota((cap, models), 0) == dest_row * slots + rank_row, 1.0, 0.0).astype(bf16)
        out = split_dot(jnp.concatenate(blocks, 1), home)
    else:
        home = jnp.where(iota((cap, models), 0) == place * slots + rank_row, 1.0, 0.0).astype(bf16)
        back = split_dot(jnp.concatenate([state_in[p] for p in range(n)], 0), home)
        out = jnp.zeros((scen, models), f32)
        for p in range(n):
            out = out + jnp.where(dest_row == p, back[p * scen : (p + 1) * scen], 0.0)
    current_ref[...] = out
    pass_on([4])

    def add_far(first, last):
        for at in range(0, width, tile):
            columns = slice(at, at + tile)
            total = voltage_ref[:, columns]
            for start in (0, halfrows):
                rows = pl.ds(pl.multiple_of((1 - top) * cap + start + first, 16), last - first)
                total = total + jnp.dot(
                    far[:, start + first : start + last], solve[rows, columns], preferred_element_type=f32
                )
            voltage_ref[:, columns] = total

    for copy in spread_far[1:4]:
        copy.wait()
    add_far(0, 3 * chunk)
    for copy in spread_far[4:]:
        copy.wait()
    add_far(3 * chunk, 4 * chunk)


def write_kernel(voltage_ref, current_ref, voltage_out, current_out, sems):
    copies = [
        pltpu.make_async_copy(voltage_ref, voltage_out, sems.at[0]),
        pltpu.make_async_copy(current_ref, current_out, sems.at[1]),
    ]
    for copy in copies:
        copy.start()
    for copy in copies:
        copy.wait()


def per_device(
    inverse,
    voltage_prev,
    line_delay,
    line_bus,
    line_impedance,
    line_past,
    model_dest,
    model_bus,
    model_gain,
    model_lag,
    model_state,
    model_source,
    switch_bus,
    switch_admittance,
):
    n = lax.axis_size("rows")
    groups = lax.axis_size("scen")
    local, width = inverse.shape
    scen = voltage_prev.shape[0]
    steps = model_source.shape[0]
    ends = line_bus.shape[1]
    models = model_bus.shape[0]
    depth_max = line_past.shape[0]
    slots = max(2, 2 * models // n)
    cap = n * slots
    f32, bf16 = jnp.float32, jnp.bfloat16
    subs = n // 2
    pad = max(128, 2 * ends)
    points = 2 * cap + pad
    cols = cap + pad
    wide = cols if pad > 2 * ends else cols + 128
    past_rows = depth_max * 2 * scen
    quarter = (16 + (steps + 1) * scen) // 4
    packed = pad == 128 and max(subs - 1, depth_max) * 2 * ends <= 128 and 4 * ends <= 128 and scen == 16
    line_rows = 8 if packed else scen
    tight = slots == 32 and n % 4 == 0 and scen == 16
    copies = 3 * (n - 1) + (steps - 2) * (subs - 1) + 36
    vmem = pl.BlockSpec(memory_space=pltpu.VMEM)
    hbm = pl.BlockSpec(memory_space=pl.ANY)
    voltage, model_current = pl.pallas_call(
        functools.partial(step_kernel, n, steps, depth_max, cap, slots, pad, packed, tight),
        out_shape=(pltpu.VMEM((scen, width), f32), pltpu.VMEM((scen, models), f32)),
        in_specs=[hbm] * 14,
        out_specs=(vmem, vmem),
        scratch_shapes=[
            pltpu.VMEM((local, width), bf16),
            pltpu.VMEM((scen, width), f32),
            pltpu.VMEM((1, ends), jnp.int32),
            pltpu.VMEM((1, ends), jnp.int32),
            pltpu.VMEM((1, ends), f32),
            pltpu.VMEM((past_rows, ends), f32),
            pltpu.VMEM((1, models), jnp.int32),
            pltpu.VMEM((1, models), jnp.int32),
            pltpu.VMEM((1, models), f32),
            pltpu.VMEM((1, models), f32),
            pltpu.VMEM((scen, models), f32),
            pltpu.VMEM((steps * scen, models), f32),
            pltpu.VMEM((2, subs, scen), jnp.int32),
            pltpu.VMEM((subs, scen), f32),
            pltpu.VMEM((8, pad), f32),
            pltpu.VMEM((8, pad), f32),
            pltpu.VMEM((scen if packed else past_rows, pad), f32),
            pltpu.VMEM((scen if packed else past_rows, pad), f32),
            pltpu.VMEM((8, 128), f32),
            pltpu.VMEM((groups - 1, 8, 128), f32),
            pltpu.VMEM((subs, 8, 256), f32),
            pltpu.VMEM((n, 8, 256), f32),
            pltpu.VMEM((subs, quarter, 256), f32),
            pltpu.VMEM((n, quarter, 256), f32),
            pltpu.VMEM((width, cols), bf16),
            pltpu.VMEM((cap + ends, local), bf16),
            pltpu.VMEM((cap + ends, width), bf16),
            pltpu.VMEM((cap // 2, width), bf16),
            pltpu.VMEM((ends, width // 2), bf16),
            pltpu.VMEM((points, width), bf16),
            pltpu.VMEM((points, points), bf16),
            pltpu.VMEM((groups * scen, width), f32),
            pltpu.VMEM((2 * scen, width), f32),
            pltpu.VMEM((2 * scen, width), f32),
            pltpu.VMEM((scen, width), f32),
            pltpu.VMEM((cap + ends, cols), bf16),
            pltpu.VMEM((cap + ends, cols), bf16),
            pltpu.VMEM((groups * scen, wide), f32),
            pltpu.VMEM((2 * scen, wide), f32),
            pltpu.VMEM((2 * scen, wide), f32),
            pltpu.VMEM((3, scen, wide), f32),
            pltpu.VMEM((scen, cap), f32),
            pltpu.VMEM((scen, cap), f32),
            pltpu.VMEM((4, cap, cap), bf16),
            pltpu.VMEM((4, ends, cols), bf16),
            pltpu.VMEM((points, points), bf16),
            pltpu.VMEM((steps - 2, subs - 1, line_rows, pad), f32),
            pltpu.VMEM((steps - 2, subs - 1, line_rows, pad), f32),
            pltpu.VMEM((n, 8, 128) if tight else (1, scen, cap), f32),
            pltpu.VMEM((n, 8, 128) if tight else (n, scen, cap), f32),
            pltpu.SemaphoreType.DMA((14,)),
            pltpu.SemaphoreType.DMA((copies, 2)),
        ],
        compiler_params=pltpu.CompilerParams(
            collective_id=0, has_side_effects=True, vmem_limit_bytes=56 * 2**20
        ),
    )(
        inverse,
        voltage_prev,
        line_delay,
        line_bus,
        line_impedance,
        line_past.reshape(past_rows, ends),
        model_dest.reshape(1, models),
        model_bus.reshape(1, models),
        model_gain.reshape(1, models),
        model_lag.reshape(1, models),
        model_state,
        model_source.reshape(steps * scen, models),
        jnp.swapaxes(switch_bus, 1, 2),
        switch_admittance.T,
    )
    return pl.pallas_call(
        write_kernel,
        out_shape=(
            jax.ShapeDtypeStruct((scen, width), f32),
            jax.ShapeDtypeStruct((scen, models), f32),
        ),
        in_specs=[vmem, vmem],
        out_specs=(hbm, hbm),
        scratch_shapes=[pltpu.SemaphoreType.DMA((2,))],
    )(pltpu.with_memory_space_constraint(voltage, pltpu.VMEM), pltpu.with_memory_space_constraint(model_current, pltpu.VMEM))


def solution(mesh):
    placed = (
        P("scen", "rows"),
        P("scen", "rows"),
        P("rows", None),
        P("rows", None),
        P("rows", None),
        P(None, None, "scen", "rows", None),
        P("rows", None),
        P("rows"),
        P("rows"),
        P("rows"),
        P("scen", "rows"),
        P(None, "scen", "rows"),
        P(None, "scen", None),
        P("scen", None),
    )
    return jax.shard_map(
        per_device,
        mesh=mesh,
        in_specs=placed,
        out_specs=(P("scen", "rows"), P("scen", "rows")),
        check_vma=False,
    )
```

```python
import functools

import jax
import jax.numpy as jnp
from jax import lax
from jax.experimental import pallas as pl
from jax.experimental.pallas import tpu as pltpu
from jax.sharding import PartitionSpec as P


def split_dot(value, selector):
    rows = value.shape[0]
    high = value.astype(jnp.bfloat16)
    rest = value - high.astype(jnp.float32)
    middle = rest.astype(jnp.bfloat16)
    low = (rest - middle.astype(jnp.float32)).astype(jnp.bfloat16)
    stacked = jnp.concatenate([high, middle, low], 0)
    out = jnp.dot(stacked, selector, preferred_element_type=jnp.float32)
    return out[:rows] + out[rows : 2 * rows] + out[2 * rows :]


def bits(value):
    return value.bit_length() - 1


def step_kernel(
    n,
    steps,
    depth_max,
    cap,
    slots,
    pad,
    packed,
    tight,
    inverse_hbm,
    prev_hbm,
    delay_hbm,
    end_hbm,
    impedance_hbm,
    past_hbm,
    dest_hbm,
    bus_hbm,
    gain_hbm,
    lag_hbm,
    state_hbm,
    source_hbm,
    switch_hbm,
    admit_hbm,
    voltage_ref,
    current_ref,
    inverse_ref,
    prev_ref,
    delay_ref,
    end_ref,
    impedance_ref,
    past_ref,
    dest_ref,
    bus_ref,
    gain_ref,
    lag_ref,
    state_ref,
    source_ref,
    switch_ref,
    admit_ref,
    head_out,
    head_in,
    past_out,
    past_in,
    switch_out,
    switch_in,
    bus_out,
    bus_in,
    model_out,
    model_in,
    col_sel,
    row_sel,
    rows_part,
    rows_mate,
    ends_mate,
    solve,
    merge,
    branch_part,
    branch_mate,
    branch_sum,
    branch_in,
    part,
    part_in,
    side,
    side_mate,
    side_out,
    side_in,
    volt_out,
    volt_in,
    quads,
    line_rows,
    matrix,
    line_out,
    line_in,
    state_out,
    state_in,
    local_sems,
    sems,
):
    f32, bf16 = jnp.float32, jnp.bfloat16
    place = lax.axis_index("rows")
    share = lax.axis_index("scen")
    subs = n // 2
    subnet, half = place // 2, place % 2
    pair = place + 1 - 2 * half
    lower = half == 0
    top, core = share // 2, share % 2
    upward = top == 0
    mate, across, corner = share + 1 - 2 * core, (share + 2) % 4, 3 - share
    scen = state_ref.shape[0]
    local, width = inverse_ref.shape
    models = dest_ref.shape[1]
    ends = end_ref.shape[1]
    count = [0]

    def remote(src, dst, device):
        at = count[0]
        count[0] += 1
        return pltpu.make_async_remote_copy(
            src_ref=src,
            dst_ref=dst,
            send_sem=sems.at[at, 0],
            recv_sem=sems.at[at, 1],
            device_id=device,
            device_id_type=pl.DeviceIdType.MESH,
        )

    barrier = pltpu.get_barrier_semaphore()
    friends = [(place, mate), (place, across), (place, corner), (pair, across)]
    friends += [((place + d) % n, share) for d in range(1, n)]
    for device in friends:
        pl.semaphore_signal(barrier, inc=1, device_id=device, device_id_type=pl.DeviceIdType.MESH)
    arrays = [
        (dest_hbm, dest_ref),
        (bus_hbm, bus_ref),
        (switch_hbm, switch_ref),
        (admit_hbm, admit_ref),
        (delay_hbm, delay_ref),
        (end_hbm, end_ref),
        (impedance_hbm, impedance_ref),
        (past_hbm, past_ref),
        (lag_hbm, lag_ref),
        (gain_hbm, gain_ref),
        (state_hbm, state_ref),
        (source_hbm, source_ref),
        (inverse_hbm, inverse_ref),
        (prev_hbm, prev_ref),
    ]
    loads = [pltpu.make_async_copy(src, dst, local_sems.at[at]) for at, (src, dst) in enumerate(arrays)]
    for copy in loads:
        copy.start()
    load_inverse, load_prev = loads[12:]
    for copy in loads[:2]:
        copy.wait()

    iota = functools.partial(lax.broadcasted_iota, jnp.int32)
    group = 128 // slots
    dest_row = dest_ref[...]
    dest = jnp.broadcast_to(dest_row.astype(f32), (models, models))
    dest_col = dest.T
    same = dest == dest_col
    rows_at, lanes_at = iota((models, models), 0), iota((models, models), 1)
    rank_col = jnp.sum(jnp.where(same & (lanes_at < rows_at), 1.0, 0.0), axis=1, keepdims=True)
    dest_col = dest_col[:, 0:1].astype(jnp.int32)
    spot = (dest_col >> 1) * 256 + (dest_col & 1) * 128 + rank_col.astype(jnp.int32)
    spot = spot + (place % group) * slots
    placing = jnp.where(iota((models, subs * 256), 1) == spot, 1.0, 0.0).astype(bf16)
    bus_row = (bus_ref[...] + (dest_row & 1) * width + 1).astype(f32)
    spread = split_dot(jnp.broadcast_to(bus_row, (16, models)), placing)
    for g in range(subs):
        bus_out[g] = spread[:8, g * 256 : (g + 1) * 256]

    pl.semaphore_wait(barrier, len(friends))
    moved_buses = []
    for d in range(1, n):
        to = (place + d) % n
        moved_buses.append(remote(bus_out.at[to // 2], bus_in.at[place], (to, share)))
    for copy in moved_buses:
        copy.start()
    bus_in[place] = bus_out[subnet]
    for copy in loads[2:8]:
        copy.wait()
    switch_out[...] = jnp.zeros_like(switch_out)
    named = iota((subs, scen), 0) == subnet
    for row, values in enumerate((switch_ref[0].astype(f32), switch_ref[1].astype(f32), admit_ref[...])):
        switch_out[row : row + 1, :scen] = jnp.sum(jnp.where(named, values, 0.0), axis=0, keepdims=True)
    head_out[...] = jnp.zeros_like(head_out)
    head_out[0:1, :ends] = delay_ref[...].astype(f32)
    head_out[1:2, :ends] = impedance_ref[...]
    head_out[2:3, :ends] = (end_ref[...] + half * width + 1).astype(f32)
    head = head_out[...]
    head_out[...] = jnp.where(lower, head, pltpu.roll(head, ends, 1))
    past_out[...] = jnp.zeros_like(past_out)
    if packed:
        scale = 2.0 / jnp.where(delay_ref[...] == 0, 1.0, impedance_ref[...])
        for k in range(depth_max):
            older = past_ref[k * 2 * scen : (k + 1) * 2 * scen, :]
            past_out[:, k * 2 * ends : (2 * k + 1) * ends] = -scale * older[:scen] - older[scen:]
    else:
        past_out[:, :ends] = past_ref[...]
    past = past_out[...]
    past_out[...] = jnp.where(lower, past, pltpu.roll(past, ends, 1))

    switches = [
        remote(switch_out, switch_in.at[at], (place, to)) for at, to in enumerate((across, mate, corner))
    ]
    for copy in switches:
        copy.start()
    head_copy = remote(head_out, head_in, (pair, share))
    head_copy.start()
    past_copy = remote(past_out, past_in, (pair, share))
    past_copy.start()

    for copy in loads[8:12]:
        copy.wait()
    lag_row = lag_ref[...]
    gain_row = (1.0 - lag_row) * gain_ref[...]
    payload = jnp.concatenate(
        [
            jnp.broadcast_to(lag_row, (8, models)),
            jnp.broadcast_to(gain_row, (8, models)),
            state_ref[...],
            source_ref[...],
        ],
        0,
    )
    quarter = payload.shape[0] // 4
    for g in range(subs):
        base = split_dot(payload, placing[:, g * 256 : (g + 1) * 256])
        for h in range(2):
            lanes = slice(h * 128, (h + 1) * 128)
            total = base[:quarter, lanes]
            for q in range(1, 4):
                total = total + pltpu.roll(base[q * quarter : (q + 1) * quarter, lanes], 32 * q, 1)
            model_out[g, :, lanes] = total
    moved_models = []
    for d in range(1, n):
        to = (place + d) % n
        moved_models.append(remote(model_out.at[to // 2], model_in.at[place], (to, share)))
    for copy in moved_models:
        copy.start()
    model_in[place] = model_out[subnet]

    for copy in switches:
        copy.wait()
    switch = switch_out[...]
    for at in range(3):
        switch = switch + pltpu.roll(switch_in[at], scen * (at + 1), 1)
    switch = jnp.concatenate([switch] * 16, 0).T
    scens = 4 * scen
    pick_a, pick_b = switch[:scens, 0:1].astype(jnp.int32), switch[:scens, 1:2].astype(jnp.int32)
    admit = switch[:scen, 2:3]
    row_ids = iota((scens, local), 1) + share * local
    picks = (jnp.where(row_ids == pick_a, 1.0, 0.0) - jnp.where(row_ids == pick_b, 1.0, 0.0)).astype(bf16)
    load_inverse.wait()
    tile = min(width, 512)
    for at in range(0, width, tile):
        branch_part[:, at : at + tile] = jnp.dot(
            picks, inverse_ref[:, at : at + tile], preferred_element_type=f32
        )
    branch_copy = remote(branch_part.at[2 * scen :], branch_mate, (place, mate))
    branch_copy.start()

    head_copy.wait()
    for copy in moved_buses:
        copy.wait()
    head = head_out[...] + head_in[...]
    pieces = []
    for h in range(2):
        for g in range(n // group):
            total = bus_in[g * group, :, h * 128 : (h + 1) * 128]
            for k in range(1, group):
                total = total + bus_in[g * group + k, :, h * 128 : (h + 1) * 128]
            pieces.append(total)
    pts = jnp.concatenate(pieces + [jnp.broadcast_to(head[2:3], (8, pad))], 1)
    pts_col = pts.T[:, 0:1].astype(jnp.int32) - 1
    pts = pts[0:1].astype(jnp.int32) - 1
    points = 2 * cap + pad
    cols = cap + pad
    own_pts = jnp.concatenate(
        [jnp.where(lower, pts[:, :cap], pts[:, cap : 2 * cap]), pts[:, 2 * cap :]], 1
    ) - half * width
    minor = jnp.where(iota((128, cols), 0) == (own_pts & 127), 1.0, 0.0).astype(bf16)
    major = own_pts >> 7
    own_rows = jnp.concatenate(
        [
            jnp.where(upward, pts_col[:cap], pts_col[cap : 2 * cap]),
            jnp.where(upward, pts_col[2 * cap : 2 * cap + ends], pts_col[2 * cap + ends : 2 * cap + 2 * ends]),
        ],
        0,
    ) - share * local
    live = cap + ends
    row_sel[...] = jnp.where(iota((live, local), 1) == own_rows, 1.0, 0.0).astype(bf16)
    for at in range(0, width, tile):
        rows_part[:, at : at + tile] = jnp.dot(
            row_sel[...], inverse_ref[:, at : at + tile], preferred_element_type=f32
        ).astype(bf16)
        if at + tile == width // 2:
            branch_copy.wait()
            branch_sum[...] = branch_part[: 2 * scen] + branch_mate[...]
            branch_across = remote(branch_sum.at[scen:], branch_in, (place, across))
            branch_across.start()
        for row in range(at // 128, (at + tile) // 128):
            chosen = jnp.where(major == row, 1.0, 0.0).astype(bf16)
            col_sel[row * 128 : (row + 1) * 128] = minor * chosen
    part[...] = jnp.dot(rows_part[...], col_sel[...], preferred_element_type=f32).astype(bf16)
    halfrows, halfwidth = cap // 2, width // 2
    own_half = pl.ds(pl.multiple_of(core * halfrows, 16), halfrows)
    mate_half = pl.ds(pl.multiple_of((1 - core) * halfrows, 16), halfrows)
    own_lanes = pl.ds(pl.multiple_of(core * halfwidth, 128), halfwidth)
    mate_lanes = pl.ds(pl.multiple_of((1 - core) * halfwidth, 128), halfwidth)
    rows_copy = remote(rows_part.at[mate_half], rows_mate, (place, mate))
    ends_copy = remote(rows_part.at[cap:, mate_lanes], ends_mate, (place, mate))
    part_copy = remote(part, part_in, (place, mate))
    part_copy.start()
    rows_copy.start()
    ends_copy.start()
    depth_part = jnp.zeros((scens, 1), f32)
    for at in range(0, width, tile):
        col_ids = iota((scens, tile), 1) + (half * width + at)
        signs = jnp.where(col_ids == pick_a, 1.0, 0.0) - jnp.where(col_ids == pick_b, 1.0, 0.0)
        depth_part = depth_part + jnp.sum(branch_part[:, at : at + tile] * signs, axis=1, keepdims=True)
    wide = side.shape[1]
    product = split_dot(branch_part[...], col_sel[...])
    if wide > cols:
        product = jnp.concatenate([product, jnp.zeros((scens, wide - cols), f32)], 1)
    side[...] = jnp.where(iota((scens, wide), 1) == wide - 1, depth_part, product)
    side_copy = remote(side.at[2 * scen :], side_mate, (place, mate))
    side_copy.start()
    load_prev.wait()
    volt_out[...] = split_dot(prev_ref[...], col_sel[:, :cap])
    volt_copy = remote(volt_out, volt_in, (pair, share))
    volt_copy.start()
    mine = top * 2 + half
    part_copy.wait()
    whole = part[...] + part_in[...]
    quads[mine] = whole[:cap, :cap]
    line_rows[mine] = whole[cap:]
    others = [(pair, across), (place, across), (pair, share)]
    theirs = [(1 - top) * 2 + 1 - half, (1 - top) * 2 + half, top * 2 + 1 - half]
    quad_copies, row_copies, sides, forwards = [], [], [], []
    for device in others:
        row_copies.append(remote(line_rows.at[mine], line_rows.at[mine], device))
        row_copies[-1].start()
    side_copy.wait()
    side_out[...] = side[: 2 * scen] + side_mate[...]
    for at, device in enumerate(others):
        rows = slice(0, scen) if at == 2 else slice(scen, 2 * scen)
        sides.append(remote(side_out.at[rows], side_in.at[at], device))
        sides[-1].start()
    for device in others:
        quad_copies.append(remote(quads.at[mine, own_half], quads.at[mine, own_half], device))
        quad_copies[-1].start()
    rows_copy.wait()
    ends_copy.wait()
    if pad > 2 * ends:
        solve[2 * cap + 2 * ends :] = jnp.zeros((pad - 2 * ends, width), bf16)
    solve_rows = pl.ds(pl.multiple_of(top * cap + core * halfrows, 16), halfrows)
    solve_ends = pl.ds(pl.multiple_of(2 * cap + top * ends, 16), ends)
    solve[solve_rows] = rows_part[own_half] + rows_mate[...]
    solve[solve_ends, own_lanes] = rows_part[cap:, own_lanes] + ends_mate[...]
    their_ends = pl.ds(pl.multiple_of(2 * cap + (1 - top) * ends, 16), ends)
    spread_rows, spread_mate, spread_far = [], [], []
    chunk = halfrows // 4
    their_parts = []
    there = solve.at[solve_ends, own_lanes]
    spread_rows.append(remote(there, there, (place, across)))
    their_parts.append(solve.at[their_ends, own_lanes])
    for at in range(4):
        first = pl.multiple_of(top * cap + core * halfrows + at * chunk, 16)
        there = solve.at[pl.ds(first, chunk)]
        spread_rows.append(remote(there, there, (place, across)))
        first = pl.multiple_of((1 - top) * cap + core * halfrows + at * chunk, 16)
        their_parts.append(solve.at[pl.ds(first, chunk)])
    for there in (solve.at[solve_rows], solve.at[solve_ends, own_lanes]):
        spread_mate.append(remote(there, there, (place, mate)))

    def pass_on(parts):
        for at in parts:
            spread_rows[at].wait()
            spread_far.append(remote(their_parts[at], their_parts[at], (place, mate)))
            spread_far[-1].start()

    for copy in spread_rows:
        copy.start()
    equal = pts == pts_col
    sub_at = iota((points, points), 0)
    leader = jnp.min(jnp.where(equal, sub_at.astype(f32), float(points)), axis=0, keepdims=True)
    leading = leader == iota((1, points), 1).astype(f32)
    merge[...] = jnp.where(equal & leading, 1.0, 0.0).astype(bf16)
    lane = iota((1, pad), 1)
    per_pair = ends // n
    partner = (lane & (ends - 1)) >> bits(per_pair)
    origin = (partner & 1) * ends + (lane >> bits(ends)) * per_pair + (lane & (per_pair - 1))
    origin = jnp.where(lane < 2 * ends, origin + subnet * (2 * per_pair), -1)
    perm = jnp.where(iota((pad, pad), 0) == origin, 1.0, 0.0).astype(bf16)
    partner = partner >> 1
    if packed:
        way, spot = lane >> bits(2 * ends), lane & (2 * ends - 1)
        to = (subnet + way + 1) & (subs - 1)
        fellow = (spot & (ends - 1)) >> bits(per_pair)
        origin = (fellow & 1) * ends + (to * 2 + (spot >> bits(ends))) * per_pair + (spot & (per_pair - 1))
        sent = (way < subs - 1) & ((fellow >> 1) == subnet)
        spread = jnp.where(iota((pad, pad), 0) == jnp.where(sent, origin, -1), 1.0, 0.0).astype(bf16)


    for copy in sides:
        copy.wait()
    near = side_out[:scen] + side_in[1]
    far = side_in[0] + side_in[2]
    rest = near[:, cap:] + far[:, cap:]
    spare = iota((scen, pad), 1) < 2 * ends
    branch = jnp.concatenate(
        [
            jnp.where(lower, near[:, :cap], far[:, :cap]),
            jnp.where(lower, far[:, :cap], near[:, :cap]),
            jnp.where(spare, rest[:, :pad], 0.0),
        ],
        1,
    )
    depth = rest[:, wide - cap - 1 : wide - cap]
    volt_copy.wait()
    own_volt, other_volt = volt_out[...], volt_in[...]
    volt = jnp.concatenate(
        [jnp.where(lower, own_volt, other_volt), jnp.where(lower, other_volt, own_volt)], 1
    )
    delays, impedance = head[0:1], head[1:2]
    admittance = 2.0 / jnp.where(delays == 0.0, 1.0, impedance)
    past_copy.wait()
    past = past_out[...] + past_in[...]
    history = []
    for k in range(depth_max):
        if packed:
            history.append(pltpu.roll(past, (pad - k * 2 * ends) % pad, 1) if k else past)
        else:
            older = past[k * 2 * scen : (k + 1) * 2 * scen]
            history.append(-admittance * older[:scen] - older[scen:])
    branch_ends, admittance_ends = branch[:, 2 * cap :], admittance
    if packed:
        branch_ends = split_dot(branch_ends, spread)
        admittance_ends = split_dot(jnp.broadcast_to(admittance, (16, pad)), spread)[:1]
    for copy in moved_models:
        copy.wait()
    band_of = iota((quarter, 128), 1) >> 5
    received = [[] for _ in range(4)]
    for h in range(2):
        for g in range(n // group):
            bands = []
            for b in range(4):
                members = [g * group + k for k in range(group) if k * slots // 32 == b]
                total = model_in[members[0], :, h * 128 : (h + 1) * 128]
                for p in members[1:]:
                    total = total + model_in[p, :, h * 128 : (h + 1) * 128]
                bands.append(total)
            for q in range(4):
                total = bands[(3 - q) % 4]
                for b in range(3):
                    total = jnp.where(band_of == b, bands[(b - q) % 4], total)
                received[q].append(pltpu.roll(total, (128 - 32 * q) % 128, 1) if q else total)
    received = jnp.concatenate([jnp.concatenate(parts, 1) for parts in received], 0)
    lag, gain = received[0:1], received[8:9]
    current = received[16 : 16 + scen]
    lines = []
    homes = []
    for step in range(steps):
        current = lag * current + gain * (received[16 + (step + 1) * scen : 16 + (step + 2) * scen] - volt)
        if step + 1 == steps:
            mine = jnp.where(lower, current[:, :cap], current[:, cap:])
            if tight:
                for p in range(n):
                    block, shift = slice(p // 4 * 128, p // 4 * 128 + 128), p % 4 * 32
                    upper = pltpu.roll(mine[:8, block], 128 - shift, 1) if shift else mine[:8, block]
                    under = pltpu.roll(mine[8:, block], (192 - shift) % 128, 1) if shift != 64 else mine[8:, block]
                    state_out[p] = jnp.where(lane < 64, upper, under)
            else:
                state_out[0] = mine
            for d in range(1, n):
                to = (place + d) % n
                homes.append(
                    remote(state_out.at[to if tight else 0], state_in.at[place], (to, share))
                )
            for copy in homes:
                copy.start()
        feed = split_dot(current, merge[: 2 * cap])
        if step + 1 == steps:
            pass_on(range(3))
        if step >= 2:
            for copy in lines[step - 2]:
                copy.wait()
            arrived = line_in[step - 2, 0]
            if packed:
                for d in range(2, subs):
                    arrived = arrived + line_in[step - 2, d - 1]
                arrived = jnp.concatenate([arrived, pltpu.roll(arrived, pad // 2, 1)], 0)
            else:
                arrived = jnp.zeros((scen, pad), f32)
                for d in range(1, subs):
                    moved = split_dot(line_in[step - 2, d - 1], perm)
                    arrived = arrived + jnp.where(partner == (subnet + subs - d) % subs, moved, 0.0)
            history.append(arrived)
        line_term = jnp.zeros((scen, pad), f32)
        for delay in range(2, depth_max + 1):
            line_term = line_term + jnp.where(delays == delay, history[step - delay + depth_max], 0.0)
        feed = feed - split_dot(line_term, merge[2 * cap :])
        rhs = feed.astype(bf16)
        term_ends = split_dot(line_term, spread) if packed else line_term
        along = jnp.sum(rhs.astype(f32) * branch, axis=1, keepdims=True)
        factor = admit * along / (1.0 + admit * depth)
        if step == 0:
            for copy in row_copies:
                copy.wait()
            matrix[2 * cap :, :] = jnp.zeros((pad, points), bf16)
            for x in range(2):
                rows = slice(2 * cap + x * ends, 2 * cap + (x + 1) * ends)
                for h in range(2):
                    matrix[rows, h * cap : (h + 1) * cap] = line_rows[2 * x + h, :, :cap]
                matrix[rows, 2 * cap :] = line_rows[2 * x, :, cap:] + line_rows[2 * x + 1, :, cap:]
            matrix[: 2 * cap, 2 * cap :] = matrix[2 * cap :, : 2 * cap].astype(f32).T.astype(bf16)
            if packed:
                matrix[:, 2 * cap :] = jnp.dot(
                    matrix[:, 2 * cap :], spread, preferred_element_type=f32
                ).astype(bf16)
        if step + 2 < steps:
            sending = jnp.dot(rhs, matrix[:, 2 * cap :], preferred_element_type=f32)
            sending = -admittance_ends * (sending - factor * branch_ends) - term_ends
            for d in range(1, subs):
                if packed:
                    upper = pltpu.roll(sending[:8], (128 - 2 * ends * (d - 1)) % 128, 1) if d > 1 else sending[:8]
                    under = pltpu.roll(sending[8:], (64 - 2 * ends * (d - 1)) % 128, 1)
                    line_out[step, d - 1] = jnp.where(lane < 64, upper, under)
                else:
                    line_out[step, d - 1] = sending
            lines.append(
                [
                    remote(
                        line_out.at[step, d - 1],
                        line_in.at[step, d - 1],
                        (((subnet + d) % subs) * 2 + half, share),
                    )
                    for d in range(1, subs)
                ]
            )
            for copy in lines[step]:
                copy.start()
        if step == 0:
            for at in range(3):
                quad_copies[at].wait_recv()
                there = quads.at[theirs[at], own_half]
                forwards.append(remote(there, there, (place, mate)))
                forwards[-1].start()
            for copy in spread_mate:
                copy.start()
            for copy in quad_copies:
                copy.wait_send()
            for copy in forwards:
                copy.wait()
            for x in range(2):
                for h in range(2):
                    matrix[x * cap : (x + 1) * cap, h * cap : (h + 1) * cap] = quads[2 * x + h]
        if step + 1 < steps:
            volt = jnp.dot(rhs, matrix[:, : 2 * cap], preferred_element_type=f32)
            volt = volt - factor * branch[:, : 2 * cap]

    pass_on([3])
    branch_across.wait()
    for copy in spread_mate + spread_far[:1]:
        copy.wait()
    near = jnp.concatenate([jnp.where(upward, rhs[:, :cap], rhs[:, cap : 2 * cap]), rhs[:, 2 * cap :]], 1)
    far = jnp.where(upward, rhs[:, cap : 2 * cap], rhs[:, :cap])
    near_rows = pl.ds(pl.multiple_of(top * cap, 16), cap)
    for at in range(0, width, tile):
        columns = slice(at, at + tile)
        product = jnp.dot(near[:, :cap], solve[near_rows, columns], preferred_element_type=f32)
        product = product + jnp.dot(near[:, cap:], solve[2 * cap :, columns], preferred_element_type=f32)
        voltage_ref[:, columns] = product - factor * (branch_sum[:scen, columns] + branch_in[:, columns])
    for copy in homes:
        copy.wait()
    rank_row = jnp.sum(jnp.where(same & (rows_at < lanes_at), 1.0, 0.0), axis=0, keepdims=True)
    rank_row = rank_row.astype(jnp.int32)
    state_in[place] = state_out[place if tight else 0]
    if tight:
        blocks = []
        for g in range(n // 4):
            upper, under = state_in[4 * g], pltpu.roll(state_in[4 * g], 64, 1)
            for k in range(1, 4):
                tile_in = state_in[4 * g + k]
                upper = jnp.where(band_of[:8] == k, pltpu.roll(tile_in, 32 * k, 1), upper)
                under = jnp.where(
                    band_of[:8] == k, pltpu.roll(tile_in, (32 * k + 64) % 128, 1) if k != 2 else tile_in, under
                )
            blocks.append(jnp.concatenate([upper, under], 0))
        home = jnp.where(iota((cap, models), 0) == dest_row * slots + rank_row, 1.0, 0.0).astype(bf16)
        out = split_dot(jnp.concatenate(blocks, 1), home)
    else:
        home = jnp.where(iota((cap, models), 0) == place * slots + rank_row, 1.0, 0.0).astype(bf16)
        back = split_dot(jnp.concatenate([state_in[p] for p in range(n)], 0), home)
        out = jnp.zeros((scen, models), f32)
        for p in range(n):
            out = out + jnp.where(dest_row == p, back[p * scen : (p + 1) * scen], 0.0)
    current_ref[...] = out
    pass_on([4])

    def add_far(first, last):
        for at in range(0, width, tile):
            columns = slice(at, at + tile)
            total = voltage_ref[:, columns]
            for start in (0, halfrows):
                rows = pl.ds(pl.multiple_of((1 - top) * cap + start + first, 16), last - first)
                total = total + jnp.dot(
                    far[:, start + first : start + last], solve[rows, columns], preferred_element_type=f32
                )
            voltage_ref[:, columns] = total

    for copy in spread_far[1:4]:
        copy.wait()
    add_far(0, 3 * chunk)
    for copy in spread_far[4:]:
        copy.wait()
    add_far(3 * chunk, 4 * chunk)


def write_kernel(voltage_ref, current_ref, voltage_out, current_out, sems):
    copies = [
        pltpu.make_async_copy(voltage_ref, voltage_out, sems.at[0]),
        pltpu.make_async_copy(current_ref, current_out, sems.at[1]),
    ]
    for copy in copies:
        copy.start()
    for copy in copies:
        copy.wait()


def per_device(
    inverse,
    voltage_prev,
    line_delay,
    line_bus,
    line_impedance,
    line_past,
    model_dest,
    model_bus,
    model_gain,
    model_lag,
    model_state,
    model_source,
    switch_bus,
    switch_admittance,
):
    n = lax.axis_size("rows")
    groups = lax.axis_size("scen")
    local, width = inverse.shape
    scen = voltage_prev.shape[0]
    steps = model_source.shape[0]
    ends = line_bus.shape[1]
    models = model_bus.shape[0]
    depth_max = line_past.shape[0]
    slots = max(2, 2 * models // n)
    cap = n * slots
    f32, bf16 = jnp.float32, jnp.bfloat16
    subs = n // 2
    pad = max(128, 2 * ends)
    points = 2 * cap + pad
    cols = cap + pad
    wide = cols if pad > 2 * ends else cols + 128
    past_rows = depth_max * 2 * scen
    quarter = (16 + (steps + 1) * scen) // 4
    packed = pad == 128 and max(subs - 1, depth_max) * 2 * ends <= 128 and 4 * ends <= 128 and scen == 16
    line_rows = 8 if packed else scen
    tight = slots == 32 and n % 4 == 0 and scen == 16
    copies = 3 * (n - 1) + (steps - 2) * (subs - 1) + 36
    vmem = pl.BlockSpec(memory_space=pltpu.VMEM)
    hbm = pl.BlockSpec(memory_space=pl.ANY)
    voltage, model_current = pl.pallas_call(
        functools.partial(step_kernel, n, steps, depth_max, cap, slots, pad, packed, tight),
        out_shape=(pltpu.VMEM((scen, width), f32), pltpu.VMEM((scen, models), f32)),
        in_specs=[hbm] * 14,
        out_specs=(vmem, vmem),
        scratch_shapes=[
            pltpu.VMEM((local, width), bf16),
            pltpu.VMEM((scen, width), f32),
            pltpu.VMEM((1, ends), jnp.int32),
            pltpu.VMEM((1, ends), jnp.int32),
            pltpu.VMEM((1, ends), f32),
            pltpu.VMEM((past_rows, ends), f32),
            pltpu.VMEM((1, models), jnp.int32),
            pltpu.VMEM((1, models), jnp.int32),
            pltpu.VMEM((1, models), f32),
            pltpu.VMEM((1, models), f32),
            pltpu.VMEM((scen, models), f32),
            pltpu.VMEM((steps * scen, models), f32),
            pltpu.VMEM((2, subs, scen), jnp.int32),
            pltpu.VMEM((subs, scen), f32),
            pltpu.VMEM((8, pad), f32),
            pltpu.VMEM((8, pad), f32),
            pltpu.VMEM((scen if packed else past_rows, pad), f32),
            pltpu.VMEM((scen if packed else past_rows, pad), f32),
            pltpu.VMEM((8, 128), f32),
            pltpu.VMEM((groups - 1, 8, 128), f32),
            pltpu.VMEM((subs, 8, 256), f32),
            pltpu.VMEM((n, 8, 256), f32),
            pltpu.VMEM((subs, quarter, 256), f32),
            pltpu.VMEM((n, quarter, 256), f32),
            pltpu.VMEM((width, cols), bf16),
            pltpu.VMEM((cap + ends, local), bf16),
            pltpu.VMEM((cap + ends, width), bf16),
            pltpu.VMEM((cap // 2, width), bf16),
            pltpu.VMEM((ends, width // 2), bf16),
            pltpu.VMEM((points, width), bf16),
            pltpu.VMEM((points, points), bf16),
            pltpu.VMEM((groups * scen, width), f32),
            pltpu.VMEM((2 * scen, width), f32),
            pltpu.VMEM((2 * scen, width), f32),
            pltpu.VMEM((scen, width), f32),
            pltpu.VMEM((cap + ends, cols), bf16),
            pltpu.VMEM((cap + ends, cols), bf16),
            pltpu.VMEM((groups * scen, wide), f32),
            pltpu.VMEM((2 * scen, wide), f32),
            pltpu.VMEM((2 * scen, wide), f32),
            pltpu.VMEM((3, scen, wide), f32),
            pltpu.VMEM((scen, cap), f32),
            pltpu.VMEM((scen, cap), f32),
            pltpu.VMEM((4, cap, cap), bf16),
            pltpu.VMEM((4, ends, cols), bf16),
            pltpu.VMEM((points, points), bf16),
            pltpu.VMEM((steps - 2, subs - 1, line_rows, pad), f32),
            pltpu.VMEM((steps - 2, subs - 1, line_rows, pad), f32),
            pltpu.VMEM((n, 8, 128) if tight else (1, scen, cap), f32),
            pltpu.VMEM((n, 8, 128) if tight else (n, scen, cap), f32),
            pltpu.SemaphoreType.DMA((14,)),
            pltpu.SemaphoreType.DMA((copies, 2)),
        ],
        compiler_params=pltpu.CompilerParams(
            collective_id=0, has_side_effects=True, vmem_limit_bytes=56 * 2**20
        ),
    )(
        inverse,
        voltage_prev,
        line_delay,
        line_bus,
        line_impedance,
        line_past.reshape(past_rows, ends),
        model_dest.reshape(1, models),
        model_bus.reshape(1, models),
        model_gain.reshape(1, models),
        model_lag.reshape(1, models),
        model_state,
        model_source.reshape(steps * scen, models),
        jnp.swapaxes(switch_bus, 1, 2),
        switch_admittance.T,
    )
    return pl.pallas_call(
        write_kernel,
        out_shape=(
            jax.ShapeDtypeStruct((scen, width), f32),
            jax.ShapeDtypeStruct((scen, models), f32),
        ),
        in_specs=[vmem, vmem],
        out_specs=(hbm, hbm),
        scratch_shapes=[pltpu.SemaphoreType.DMA((2,))],
    )(pltpu.with_memory_space_constraint(voltage, pltpu.VMEM), pltpu.with_memory_space_constraint(model_current, pltpu.VMEM))


def solution(mesh):
    placed = (
        P("scen", "rows"),
        P("scen", "rows"),
        P("rows", None),
        P("rows", None),
        P("rows", None),
        P(None, None, "scen", "rows", None),
        P("rows", None),
        P("rows"),
        P("rows"),
        P("rows"),
        P("scen", "rows"),
        P(None, "scen", "rows"),
        P(None, "scen", None),
        P("scen", None),
    )
    return jax.shard_map(
        per_device,
        mesh=mesh,
        in_specs=placed,
        out_specs=(P("scen", "rows"), P("scen", "rows")),
        check_vma=False,
    )
```
